32 devices in a mesh: dom: 8 (over z, y), rows: 4 (over x, core).
Axes of the slice: x: 2, y: 2, z: 4, core: 2. Of those that a mesh axis runs over, the one named last changes fastest.
Arguments:
- images: bfloat16 [3584, 25600], P('dom', 'rows'), may hold values from -6 to 6
- panels: bfloat16 [16, 25600, 256], P('dom', 'rows')
- mean_panels: float32 [16, 25600], P('dom', 'rows'), may hold values from -6 to 6
- ctf_table: float32 [16, 25600], P(None, 'rows'), may hold values from -1 to 1
- pose_bin: int32 [3584], P('dom'), may hold values from 0 to 1
- ctf_group: int32 [3584], P('dom'), may hold values from 0 to 15
Outputs:
- scores: float32 [3584, 256], P('dom')
- factor: float32 [256, 256], replicated
The draws below stay inside these ranges and needn't reach their ends.
All inputs are finite; a program needn't handle non-finite values.
Results may differ from the reference program's by a relative error of at most 0.003.
Values sent between devices are 32-bit elements; how exact they have to be, the bound alone decides.
A program may use at most 128 MiB of HBM per device.

```python
import jax
import jax.numpy as jnp
from jax import lax

PROBES = 256
PART_DEV = 448
BIN_DEV = 2
GROUPS = 16
PIX = 25600
PARTICLES = 3584
BINS = 16
N_DOM = 8


def draw_panels(key, part):

    def one_bin(index):
        bin_key = jax.random.fold_in(key, index)
        key_common, key_single = jax.random.split(bin_key)
        common = jax.random.normal(key_common, (PIX, 1), jnp.float32)
        single = jax.random.normal(key_single, (PIX, PROBES + 2), jnp.float32)
        shared_weight = 0.6
        blended = shared_weight * common + single[:, 0:PROBES] + 0.8 * single[:, 1:PROBES + 1] + 0.5 * single[:, 2:PROBES + 2]
        spread = (1.89 + shared_weight * shared_weight) ** 0.5
        return blended * (1.0 / (spread * PIX ** 0.5))
    return lax.map(one_bin, jnp.arange(BINS, dtype=jnp.int32)).astype(jnp.bfloat16)


def plant(result, rng, smallest, top_value):
    longest = result.shape.index(max(result.shape))
    spots = []
    for shift in (0, 1):
        where = [jax.random.randint(jax.random.fold_in(rng, axis), (), 0, length) for axis, length in enumerate(result.shape)]
        where[longest] = (where[longest] + shift) % result.shape[longest]
        spots.append(tuple(where))
    return result.at[spots[0]].set(smallest).at[spots[1]].set(top_value)


def steps_of(rng, dims, cuts, least, top_value):
    def one(dim, shards_of):
        draws = jax.random.uniform(jax.random.fold_in(jax.random.fold_in(rng, 6), dim), (shards_of,), jnp.float32, least / len(cuts), top_value / len(cuts))
        return jnp.repeat(jnp.exp(draws), dims[dim] // shards_of).reshape((-1,) + (1,) * (len(dims) - dim - 1))

    gain = one(*cuts[0])
    for cut in cuts[1:]:
        gain = gain * one(*cut)
    return gain


def centred(stream_key, shape, scale, bound, cuts=(), kind=jnp.bfloat16):
    level = steps_of(stream_key, shape, cuts, -0.22, 0.18) if cuts else 1.0
    drawn = jax.random.normal(stream_key, shape, jnp.float32) * scale * level
    return jnp.minimum(jnp.maximum(drawn, -bound), bound).astype(kind)


def setup_inputs(seed: int = 0) -> dict:
    splits = jax.random.split(jax.random.key(seed), 7)
    return {
        "images": centred(splits[0], (PARTICLES, PIX), 1.0, 6.0, ((0, 8), (1, 4))),
        "panels": draw_panels(jax.random.fold_in(splits[6], 71), 0),
        "mean_panels": centred(splits[2], (BINS, PIX), 1.0, 6.0, ((0, 8), (1, 4)), jnp.float32),
        "ctf_table": jnp.clip(jax.random.uniform(splits[3], (GROUPS, PIX), jnp.float32, -1.0, 1.0) * steps_of(splits[3], (GROUPS, PIX), ((1, 4),), -0.4, 0.0), -1.0, 1.0),
        "pose_bin": plant(jax.random.randint(splits[4], (PARTICLES,), 0, BIN_DEV), jax.random.fold_in(splits[4], 1), 0, BIN_DEV - 1).astype(jnp.int32),
        "ctf_group": plant(jax.random.randint(splits[5], (PARTICLES,), 0, GROUPS), jax.random.fold_in(splits[5], 1), 0, GROUPS - 1).astype(jnp.int32),
    }


def high_dot(left, right):
    return jnp.dot(left, right, precision=lax.Precision.HIGHEST, preferred_element_type=jnp.float32)

def cholesky_small(matrix):
    order = matrix.shape[0]
    places = jnp.arange(order, dtype=jnp.int32)

    def column_step(index, carry):
        work, lower = carry
        index = jnp.asarray(index).astype(jnp.int32)
        column = lax.dynamic_slice_in_dim(work, index, 1, 1)[:, 0]
        pivot = jnp.sqrt(lax.dynamic_slice_in_dim(column, index, 1, 0)[0])
        below = jnp.where(places > index, column / pivot, jnp.zeros_like(column))
        filled = below + jnp.where(places == index, pivot, jnp.zeros_like(column))
        lower = lower + filled[:, None] * (places == index).astype(matrix.dtype)[None, :]
        work = work - below[:, None] * below[None, :]
        return (work, lower)
    return lax.fori_loop(0, order, column_step, (matrix, jnp.zeros_like(matrix)))[1]

def inverse_small(lower):
    order = lower.shape[0]
    places = jnp.arange(order, dtype=jnp.int32)

    def row_step(index, inverse):
        index = jnp.asarray(index).astype(jnp.int32)
        row_lower = lax.dynamic_slice_in_dim(lower, index, 1, 0)[0]
        pivot = lax.dynamic_slice_in_dim(row_lower, index, 1, 0)[0]
        unit = (places == index).astype(lower.dtype)
        solved = (unit - high_dot(row_lower, inverse)) / pivot
        return inverse + unit[:, None] * solved[None, :]
    return lax.fori_loop(0, order, row_step, jnp.zeros_like(lower))

def assemble(top_left, bottom_left, bottom_right):
    half = top_left.shape[0]
    rest = bottom_right.shape[0]
    upper_part = jnp.concatenate([top_left, jnp.zeros((half, rest), top_left.dtype)], axis=1)
    lower_part = jnp.concatenate([bottom_left, bottom_right], axis=1)
    return jnp.concatenate([upper_part, lower_part], axis=0)

def cholesky_pair(matrix):
    order = matrix.shape[0]
    if order <= 16:
        lower = cholesky_small(matrix)
        return (lower, inverse_small(lower))
    half = order // 2
    lower_a, inverse_a = cholesky_pair(matrix[:half, :half])
    below = high_dot(matrix[half:, :half], inverse_a.T)
    schur = matrix[half:, half:] - high_dot(below, below.T)
    lower_b, inverse_b = cholesky_pair(schur)
    inverse_mid = -high_dot(inverse_b, high_dot(below, inverse_a))
    return (assemble(lower_a, below, lower_b), assemble(inverse_a, inverse_mid, inverse_b))

def lower_inverse(lower):
    order = lower.shape[0]
    if order <= 16:
        return inverse_small(lower)
    half = order // 2
    inverse_a = lower_inverse(lower[:half, :half])
    inverse_b = lower_inverse(lower[half:, half:])
    inverse_mid = -high_dot(inverse_b, high_dot(lower[half:, :half], inverse_a))
    return assemble(inverse_a, inverse_mid, inverse_b)

def weighted_block(images_block, pose_block, group_block, panel_block, mean_block, ctf_table):
    ctf_rows = jnp.take(ctf_table, group_block.astype(jnp.int32), axis=0)
    mean_rows = jnp.take(mean_block, pose_block.astype(jnp.int32), axis=0)
    weighted = (ctf_rows * (images_block.astype(jnp.float32) - ctf_rows * mean_rows)).astype(jnp.bfloat16)
    coeffs = jnp.zeros((images_block.shape[0], panel_block.shape[2]), jnp.float32)
    for which in range(BIN_DEV):
        chosen = jnp.where((pose_block == which)[:, None], weighted, jnp.zeros_like(weighted))
        coeffs = coeffs + jnp.dot(chosen, panel_block[which], preferred_element_type=jnp.float32)
    return coeffs

def reference(images, panels, mean_panels, ctf_table, pose_bin, ctf_group):
    images_r = images.reshape(N_DOM, PART_DEV, PIX)
    pose_r = pose_bin.reshape(N_DOM, PART_DEV)
    group_r = ctf_group.reshape(N_DOM, PART_DEV)
    panels_r = panels.reshape(N_DOM, BIN_DEV, PIX, PROBES)
    means_r = mean_panels.reshape(N_DOM, BIN_DEV, PIX)

    def one_block(pieces):
        return weighted_block(pieces[0], pieces[1], pieces[2], pieces[3], pieces[4], ctf_table)
    coeffs = lax.map(one_block, (images_r, pose_r, group_r, panels_r, means_r)).reshape(PARTICLES, PROBES)
    gram = high_dot(coeffs.T, coeffs) / PARTICLES
    lower, inverse = cholesky_pair(gram)
    scores = jnp.dot(coeffs, inverse.T, precision=lax.Precision.HIGHEST)
    return (scores, lower.T)
```

```python
import functools

import jax
import jax.numpy as jnp
from jax import lax
from jax.experimental import pallas as pl
from jax.experimental.pallas import tpu as pltpu
from jax.sharding import PartitionSpec as P

F32 = jnp.float32
BF16 = jnp.bfloat16


def dot_f32(left, right, dims):
    return lax.dot_general(
        left, right, (dims, ((), ())), precision=lax.Precision.HIGHEST, preferred_element_type=F32
    )


def widen(column, lanes):
    return jnp.concatenate([column] * (lanes // 128), axis=1)


SIZE = 64
PANEL = 16


def factor_block(block):
    lane = lax.broadcasted_iota(jnp.int32, (8, 2 * SIZE), 1)
    sub = lax.broadcasted_iota(jnp.int32, (8, 2 * SIZE), 0)
    tiles = []
    for t in range(SIZE // 8):
        unit = (lane == sub + (8 * t + SIZE)).astype(F32)
        part = jnp.concatenate([block[8 * t : 8 * t + 8], jnp.zeros((8, SIZE), F32)], axis=1)
        tiles.append(part + unit)
    count = len(tiles)
    pivots = [jnp.ones((8, 2 * SIZE), F32) for _ in range(count)]
    for base in range(0, SIZE, PANEL):
        first = base // 8
        cols = [
            [None] * first
            + [jnp.broadcast_to(tiles[t][:, base + j : base + j + 1], (8, 2 * SIZE)) for t in range(first, count)]
            for j in range(PANEL)
        ]
        for j in range(PANEL):
            k = base + j
            row, here = k % 8, k // 8
            pivot = cols[j][here][row : row + 1]
            inverse = 1.0 / pivot
            pivots[here] = jnp.where(sub == row, pivot, pivots[here])
            scale = [None] * count
            for t in range(here, count):
                scale[t] = cols[j][t] * inverse
            scale[here] = jnp.where(sub > row, scale[here], 0.0)
            for later in range(j + 1, PANEL):
                value = cols[later][here][row : row + 1]
                for t in range(here, count):
                    cols[later][t] = cols[later][t] - scale[t] * value
            line = tiles[here][row : row + 1]
            for t in range(here, count):
                tiles[t] = tiles[t] - scale[t] * line
    done = []
    for t in range(count):
        keep = (lane >= SIZE) | (lane >= sub + 8 * t)
        done.append(jnp.where(keep, tiles[t] * lax.rsqrt(pivots[t]), 0.0))
    return jnp.concatenate(done, axis=0)


def finish_kernel(particles, gram, coeffs, scores, factor, work, side):
    order = gram.shape[0]
    work[...] = gram[...] * (1.0 / particles)
    spot = lax.broadcasted_iota(jnp.int32, (order, order), 0)
    side[...] = (spot == lax.broadcasted_iota(jnp.int32, (order, order), 1)).astype(F32)
    for start in range(0, order, SIZE):
        stop = start + SIZE
        both = factor_block(work[start:stop, start:stop])
        upper, lower = both[:, :SIZE], both[:, SIZE:]
        if start:
            factor[start:stop, :start] = jnp.zeros((SIZE, start), F32)
        factor[start:stop, start:stop] = upper
        reach = -(-stop // 128) * 128
        row_side = dot_f32(lower, side[start:stop, :reach], ((1,), (0,)))
        side[start:stop, :reach] = row_side
        if stop < order:
            from_col = stop // 128 * 128
            row_work = dot_f32(lower, work[start:stop, from_col:], ((1,), (0,)))
            right = row_work[:, stop - from_col :]
            factor[start:stop, stop:] = right
            work[stop:, from_col:] = work[stop:, from_col:] - dot_f32(right, row_work, ((0,), (0,)))
            side[stop:, :reach] = side[stop:, :reach] - dot_f32(right, row_side, ((0,), (0,)))
    scores[...] = dot_f32(coeffs[...], side[...], ((1,), (1,)))


def finish(gram, coeffs, particles):
    order = gram.shape[0]
    return pl.pallas_call(
        functools.partial(finish_kernel, particles),
        in_specs=[pl.BlockSpec(memory_space=pltpu.VMEM)] * 2,
        out_specs=[pl.BlockSpec(memory_space=pltpu.VMEM)] * 2,
        out_shape=[jax.ShapeDtypeStruct(coeffs.shape, F32), jax.ShapeDtypeStruct((order, order), F32)],
        scratch_shapes=[pltpu.VMEM((order, order), F32)] * 2,
        name="finish",
    )(gram, coeffs)


MESH = pl.DeviceIdType.MESH
BLOCKS = 2


def gather_kernel(n_rows, n_dom, chunk, images, panels, means, table, pose, group, coeffs, gram, *scratch):
    img, pan, mea, tab, pick, mask, acc, part, near, held, far, wide, give, take = scratch[:14]
    load_small, load_img, load_pan, pair_send, pair_recv, far_send, far_recv = scratch[14:21]
    back_send, back_recv, dom_send, dom_recv, all_send, all_recv = scratch[21:]
    row, dom = lax.axis_index("rows"), lax.axis_index("dom")
    side, pair = row % 2, row // 2
    other = 1 - side
    partner = pair * 2 + other
    across = (1 - pair) * 2 + other
    own = (side + pair) % 2
    rows, pixels = images.shape
    bins, groups = panels.shape[0], table.shape[0]
    order = panels.shape[2]
    steps = pixels // chunk
    block = rows // BLOCKS
    half = block // 2
    world = n_rows * n_dom
    ring = 2 * n_dom
    spot = dom * 2 + side
    flat = dom * n_rows + row
    piece = order // (2 * ring)

    def to(source, target, send, recv, place):
        return pltpu.make_async_remote_copy(
            src_ref=source, dst_ref=target, send_sem=send, recv_sem=recv, device_id=place, device_id_type=MESH
        )

    def local(source, target, sem):
        copy = pltpu.make_async_copy(source, target, sem)
        copy.start()
        return copy

    small = [local(table, tab, load_small.at[0]), local(means, mea, load_small.at[1])]
    weights, pictures = [], [[], []]
    for b in range(BLOCKS):
        for k in range(steps):
            px, at = pl.ds(k * chunk, chunk), pl.ds(b * block, block)
            if b == 0:
                weights.append([local(panels.at[w, px], pan.at[w, px], load_pan.at[w, k]) for w in range(bins)])
            pictures[b].append(local(images.at[at, px], img.at[at, px], load_img.at[b, k]))

    barrier = pltpu.get_barrier_semaphore()

    def greet(step, carry):
        there = (flat + step) % world
        pl.semaphore_signal(
            barrier, inc=1, device_id=(there // n_rows, there % n_rows), device_id_type=MESH
        )
        return carry

    lax.fori_loop(1, world, greet, 0)

    place = lax.broadcasted_iota(jnp.int32, (128, rows), 0)
    hot = (place % groups == group[...]) & (place < 3 * groups)
    pick[...] = jnp.transpose(hot.astype(F32)).astype(BF16)
    mask[...] = jnp.transpose(jnp.broadcast_to(pose[...].astype(F32), (128, rows)))
    for copy in small:
        copy.wait()

    def project(b, k):
        at, px = pl.ds(b * block, block), pl.ds(k * chunk, chunk)
        if b == 0:
            for copy in weights[k]:
                copy.wait()
        pictures[b][k].wait()
        exact = tab[:, px]
        high = exact.astype(BF16)
        left = exact - high.astype(F32)
        mid = left.astype(BF16)
        low = (left - mid.astype(F32)).astype(BF16)
        fill = jnp.zeros((128 - 3 * groups, chunk), BF16)
        parts = jnp.concatenate([high, mid, low, fill], axis=0)
        ctf = jnp.dot(pick[at, :], parts, preferred_element_type=F32)
        second = widen(mask[at, :], chunk) > 0.5
        mean = jnp.where(second, mea[1:2, px], mea[0:1, px])
        weighted = (ctf * (img[at, px].astype(F32) - ctf * mean)).astype(BF16)
        for which in range(2):
            value = jnp.dot(weighted, pan[which, px, :], preferred_element_type=F32)
            if k:
                value = acc[which] + value
            acc[which] = value

    def mine(b, which):
        return pl.ds(pl.multiple_of(b * block + which * half, 8), half)

    first, second, third = [], [], []

    def pair_start(b):
        part[pl.ds(b * block, block), :] = jnp.where(widen(mask[pl.ds(b * block, block), :], order) > 0.5, acc[1], acc[0])
        if b == 0:
            pl.semaphore_wait(barrier, world - 1)
        first.append(to(part.at[mine(b, 1 - own)], near.at[b], pair_send.at[b], pair_recv.at[b], (dom, partner)))
        first[b].start()

    def pair_finish(b):
        first[b].wait_recv()
        held[b] = part[mine(b, own), :] + near[b]
        second.append(to(held.at[b], far.at[b], far_send.at[b], far_recv.at[b], (dom, across)))
        second[b].start()

    columns = pl.ds(pl.multiple_of(pair * (order // 2), 128), order // 2)

    def square(b):
        second[b].wait_recv()
        coeffs[mine(b, own), :] = held[b] + far[b]
        ours = coeffs.at[mine(b, own)]
        third.append(to(ours, ours, back_send.at[b], back_recv.at[b], (dom, partner)))
        third[b].start()
        return dot_f32(coeffs[mine(b, own), columns], coeffs[mine(b, own), :], ((0,), (0,)))

    for k in range(steps):
        project(0, k)
    pair_start(0)
    for k in range(steps):
        project(1, k)
        if k == min(1, steps - 1):
            pair_finish(0)
    pair_start(1)
    pair_finish(1)
    wide[...] = square(0)
    wide[...] += square(1)
    for j in range(ring):
        give[j] = wide[j * piece : (j + 1) * piece, :]

    def deal(step):
        there = (spot + step) % ring
        return to(
            give.at[there], take.at[spot], dom_send.at[step - 1], dom_recv.at[step - 1],
            (there // 2, pair * 2 + there % 2),
        )

    def spread(step):
        there = (flat + step) % world
        ours = gram.at[pair, spot]
        return to(
            ours, ours, all_send.at[step - 1], all_recv.at[step - 1], (there // n_rows, there % n_rows)
        )

    def each(count, action):
        def one(step, carry):
            action(step)
            return carry

        lax.fori_loop(1, count, one, 0)

    each(ring, lambda step: deal(step).start())
    take[spot] = give[spot]
    each(ring, lambda step: deal(step).wait_recv())
    total = take[0]
    for j in range(1, ring):
        total = total + take[j]
    gram[pair, spot] = total
    each(world, lambda step: spread(step).start())
    for copy in third:
        copy.wait_recv()
    for copy in first + second + third:
        copy.wait_send()
    each(ring, lambda step: deal(step).wait_send())
    each(world, lambda step: spread(step).wait_recv())
    each(world, lambda step: spread(step).wait_send())


def gather(images, panels, means, table, pose, group):
    n_rows, n_dom = lax.axis_size("rows"), lax.axis_size("dom")
    rows, pixels = images.shape
    bins, _, order = panels.shape
    chunk = 1280 if pixels % 1280 == 0 else 128
    steps = pixels // chunk
    block = rows // BLOCKS
    ring = 2 * n_dom
    piece = order // (2 * ring)
    dma = pltpu.SemaphoreType.DMA
    swap = pltpu.VMEM((BLOCKS, block // 2, order), F32)
    coeffs, gram = pl.pallas_call(
        functools.partial(gather_kernel, n_rows, n_dom, chunk),
        in_specs=[pl.BlockSpec(memory_space=pl.ANY)] * 4 + [pl.BlockSpec(memory_space=pltpu.VMEM)] * 2,
        out_specs=[pl.BlockSpec(memory_space=pltpu.VMEM)] * 2,
        out_shape=[
            jax.ShapeDtypeStruct((rows, order), F32),
            jax.ShapeDtypeStruct((2, ring, piece, order), F32),
        ],
        scratch_shapes=[
            pltpu.VMEM(images.shape, BF16),
            pltpu.VMEM(panels.shape, BF16),
            pltpu.VMEM(means.shape, F32),
            pltpu.VMEM(table.shape, F32),
            pltpu.VMEM((rows, 128), BF16),
            pltpu.VMEM((rows, 128), F32),
            pltpu.VMEM((bins, block, order), F32),
            pltpu.VMEM((rows, order), F32),
            swap,
            swap,
            swap,
            pltpu.VMEM((order // 2, order), F32),
            pltpu.VMEM((ring, piece, order), F32),
            pltpu.VMEM((ring, piece, order), F32),
            dma((2,)),
            dma((BLOCKS, steps)),
            dma((bins, steps)),
        ]
        + [dma((BLOCKS,))] * 6
        + [dma((ring - 1,))] * 2
        + [dma((n_rows * n_dom - 1,))] * 2,
        compiler_params=pltpu.CompilerParams(
            collective_id=0, has_side_effects=True, vmem_limit_bytes=60 * 2**20
        ),
        name="gather",
    )(images, panels, means, table, pose.reshape(1, rows), group.reshape(1, rows))
    return coeffs, gram.reshape(order, order)


def body(images, panels, mean_panels, ctf_table, pose_bin, ctf_group):
    particles = images.shape[0] * lax.axis_size("dom")
    coeffs, gram = gather(images, panels, mean_panels, ctf_table, pose_bin, ctf_group)
    return tuple(finish(gram, coeffs, particles))


def solution(mesh):
    placed = (
        P("dom", "rows"),
        P("dom", "rows", None),
        P("dom", "rows"),
        P(None, "rows"),
        P("dom"),
        P("dom"),
    )
    return jax.shard_map(
        body, mesh=mesh, in_specs=placed, out_specs=(P("dom", None), P()), check_vma=False
    )
```

```python
import functools

import jax
import jax.numpy as jnp
from jax import lax
from jax.experimental import pallas as pl
from jax.experimental.pallas import tpu as pltpu
from jax.sharding import PartitionSpec as P

F32 = jnp.float32
BF16 = jnp.bfloat16


def dot_f32(left, right, dims):
    return lax.dot_general(
        left, right, (dims, ((), ())), precision=lax.Precision.HIGHEST, preferred_element_type=F32
    )


def widen(column, lanes):
    return jnp.concatenate([column] * (lanes // 128), axis=1)


SIZE = 64
PANEL = 16


def factor_block(block):
    lane = lax.broadcasted_iota(jnp.int32, (8, 2 * SIZE), 1)
    sub = lax.broadcasted_iota(jnp.int32, (8, 2 * SIZE), 0)
    tiles = []
    for t in range(SIZE // 8):
        unit = (lane == sub + (8 * t + SIZE)).astype(F32)
        part = jnp.concatenate([block[8 * t : 8 * t + 8], jnp.zeros((8, SIZE), F32)], axis=1)
        tiles.append(part + unit)
    count = len(tiles)
    pivots = [jnp.ones((8, 2 * SIZE), F32) for _ in range(count)]
    for base in range(0, SIZE, PANEL):
        first = base // 8
        cols = [
            [None] * first
            + [jnp.broadcast_to(tiles[t][:, base + j : base + j + 1], (8, 2 * SIZE)) for t in range(first, count)]
            for j in range(PANEL)
        ]
        for j in range(PANEL):
            k = base + j
            row, here = k % 8, k // 8
            pivot = cols[j][here][row : row + 1]
            inverse = 1.0 / pivot
            pivots[here] = jnp.where(sub == row, pivot, pivots[here])
            scale = [None] * count
            for t in range(here, count):
                scale[t] = cols[j][t] * inverse
            scale[here] = jnp.where(sub > row, scale[here], 0.0)
            for later in range(j + 1, PANEL):
                value = cols[later][here][row : row + 1]
                for t in range(here, count):
                    cols[later][t] = cols[later][t] - scale[t] * value
            line = tiles[here][row : row + 1]
            for t in range(here, count):
                tiles[t] = tiles[t] - scale[t] * line
    done = []
    for t in range(count):
        keep = (lane >= SIZE) | (lane >= sub + 8 * t)
        done.append(jnp.where(keep, tiles[t] * lax.rsqrt(pivots[t]), 0.0))
    return jnp.concatenate(done, axis=0)


def finish_kernel(particles, gram, coeffs, scores, factor, work, side):
    order = gram.shape[0]
    work[...] = gram[...] * (1.0 / particles)
    spot = lax.broadcasted_iota(jnp.int32, (order, order), 0)
    side[...] = (spot == lax.broadcasted_iota(jnp.int32, (order, order), 1)).astype(F32)
    for start in range(0, order, SIZE):
        stop = start + SIZE
        both = factor_block(work[start:stop, start:stop])
        upper, lower = both[:, :SIZE], both[:, SIZE:]
        if start:
            factor[start:stop, :start] = jnp.zeros((SIZE, start), F32)
        factor[start:stop, start:stop] = upper
        reach = -(-stop // 128) * 128
        row_side = dot_f32(lower, side[start:stop, :reach], ((1,), (0,)))
        side[start:stop, :reach] = row_side
        if stop < order:
            from_col = stop // 128 * 128
            row_work = dot_f32(lower, work[start:stop, from_col:], ((1,), (0,)))
            right = row_work[:, stop - from_col :]
            factor[start:stop, stop:] = right
            work[stop:, from_col:] = work[stop:, from_col:] - dot_f32(right, row_work, ((0,), (0,)))
            side[stop:, :reach] = side[stop:, :reach] - dot_f32(right, row_side, ((0,), (0,)))
    scores[...] = dot_f32(coeffs[...], side[...], ((1,), (1,)))


def finish(gram, coeffs, particles):
    order = gram.shape[0]
    return pl.pallas_call(
        functools.partial(finish_kernel, particles),
        in_specs=[pl.BlockSpec(memory_space=pltpu.VMEM)] * 2,
        out_specs=[pl.BlockSpec(memory_space=pltpu.VMEM)] * 2,
        out_shape=[jax.ShapeDtypeStruct(coeffs.shape, F32), jax.ShapeDtypeStruct((order, order), F32)],
        scratch_shapes=[pltpu.VMEM((order, order), F32)] * 2,
        name="finish",
    )(gram, coeffs)


MESH = pl.DeviceIdType.MESH
BLOCKS = 2


def gather_kernel(n_rows, n_dom, chunk, images, panels, means, table, pose, group, coeffs, gram, *scratch):
    img, pan, mea, tab, pick, mask, acc, part, near, held, far, wide, give, take, sems = scratch
    row, dom = lax.axis_index("rows"), lax.axis_index("dom")
    side, pair = row % 2, row // 2
    other = 1 - side
    partner = pair * 2 + other
    across = (1 - pair) * 2 + other
    own = (side + pair) % 2
    rows, pixels = images.shape
    bins, groups = panels.shape[0], table.shape[0]
    order = panels.shape[2]
    steps = pixels // chunk
    block = rows // BLOCKS
    half = block // 2
    world = n_rows * n_dom
    ring = 2 * n_dom
    spot = dom * 2 + side
    flat = dom * n_rows + row
    piece = order // (2 * ring)
    links = 2 + steps * (bins + BLOCKS)
    pair_send, pair_recv, far_send, far_recv, back_send, back_recv = range(links, links + 6 * BLOCKS, BLOCKS)
    dom_send, dom_recv, all_send, all_recv = range(links + 6 * BLOCKS, links + 6 * BLOCKS + 4)

    def to(source, target, send, recv, place):
        return pltpu.make_async_remote_copy(
            src_ref=source, dst_ref=target, send_sem=sems.at[send], recv_sem=sems.at[recv], device_id=place, device_id_type=MESH
        )

    def local(source, target, sem):
        copy = pltpu.make_async_copy(source, target, sems.at[sem])
        copy.start()
        return copy

    small = [local(table, tab, 0), local(means, mea, 1)]
    weights, pictures = [], [[], []]
    for b in range(BLOCKS):
        for k in range(steps):
            px, at = pl.ds(k * chunk, chunk), pl.ds(b * block, block)
            if b == 0:
                weights.append([local(panels.at[w, px], pan.at[w, px], 2 + w * steps + k) for w in range(bins)])
            pictures[b].append(local(images.at[at, px], img.at[at, px], 2 + (bins + b) * steps + k))

    barrier = pltpu.get_barrier_semaphore()

    def greet(step, carry):
        there = (flat + step) % world
        pl.semaphore_signal(
            barrier, inc=1, device_id=(there // n_rows, there % n_rows), device_id_type=MESH
        )
        return carry

    lax.fori_loop(1, world, greet, 0)

    place = lax.broadcasted_iota(jnp.int32, (128, rows), 0)
    hot = (place % groups == group[...]) & (place < 3 * groups)
    pick[...] = jnp.transpose(hot.astype(F32)).astype(BF16)
    mask[...] = jnp.transpose(jnp.broadcast_to(pose[...].astype(F32), (128, rows)))
    for copy in small:
        copy.wait()

    def project(b, k):
        at, px = pl.ds(b * block, block), pl.ds(k * chunk, chunk)
        if b == 0:
            for copy in weights[k]:
                copy.wait()
        pictures[b][k].wait()
        exact = tab[:, px]
        high = exact.astype(BF16)
        left = exact - high.astype(F32)
        mid = left.astype(BF16)
        low = (left - mid.astype(F32)).astype(BF16)
        fill = jnp.zeros((128 - 3 * groups, chunk), BF16)
        parts = jnp.concatenate([high, mid, low, fill], axis=0)
        ctf = jnp.dot(pick[at, :], parts, preferred_element_type=F32)
        second = widen(mask[at, :], chunk) > 0.5
        mean = jnp.where(second, mea[1:2, px], mea[0:1, px])
        weighted = (ctf * (img[at, px].astype(F32) - ctf * mean)).astype(BF16)
        for which in range(2):
            value = jnp.dot(weighted, pan[which, px, :], preferred_element_type=F32)
            if k:
                value = acc[which] + value
            acc[which] = value

    def mine(b, which):
        return pl.ds(pl.multiple_of(b * block + which * half, 8), half)

    first, second, third = [], [], []

    def pair_start(b):
        part[pl.ds(b * block, block), :] = jnp.where(widen(mask[pl.ds(b * block, block), :], order) > 0.5, acc[1], acc[0])
        if b == 0:
            pl.semaphore_wait(barrier, world - 1)
        first.append(to(part.at[mine(b, 1 - own)], near.at[b], pair_send + b, pair_recv + b, (dom, partner)))
        first[b].start()

    def pair_finish(b):
        first[b].wait_recv()
        held[b] = part[mine(b, own), :] + near[b]
        second.append(to(held.at[b], far.at[b], far_send + b, far_recv + b, (dom, across)))
        second[b].start()

    columns = pl.ds(pl.multiple_of(pair * (order // 2), 128), order // 2)

    def square(b):
        second[b].wait_recv()
        coeffs[mine(b, own), :] = held[b] + far[b]
        ours = coeffs.at[mine(b, own)]
        third.append(to(ours, ours, back_send + b, back_recv + b, (dom, partner)))
        third[b].start()
        return dot_f32(coeffs[mine(b, own), columns], coeffs[mine(b, own), :], ((0,), (0,)))

    for k in range(steps):
        project(0, k)
    pair_start(0)
    for k in range(steps):
        project(1, k)
        if k == min(1, steps - 1):
            pair_finish(0)
    pair_start(1)
    pair_finish(1)
    wide[...] = square(0)
    wide[...] += square(1)
    for j in range(ring):
        give[j] = wide[j * piece : (j + 1) * piece, :]

    def deal(step):
        there = (spot + step) % ring
        return to(give.at[there], take.at[spot], dom_send, dom_recv, (there // 2, pair * 2 + there % 2))

    def spread(step):
        there = (flat + step) % world
        ours = gram.at[pair * ring + spot]
        return to(ours, ours, all_send, all_recv, (there // n_rows, there % n_rows))

    def each(count, action):
        def one(step, carry):
            action(step)
            return carry

        lax.fori_loop(1, count, one, 0)

    each(ring, lambda step: deal(step).start())
    take[spot] = give[spot]
    others = take.at[pl.ds(0, ring - 1)]
    dealt = to(others, others, dom_send, dom_recv, (dom, partner))
    dealt.wait_recv()
    total = take[0]
    for j in range(1, ring):
        total = total + take[j]
    gram[pair * ring + spot] = total
    each(world, lambda step: spread(step).start())
    for copy in third:
        copy.wait_recv()
    for copy in first + second + third:
        copy.wait_send()
    dealt.wait_send()
    others = gram.at[pl.ds(0, world - 1)]
    spread_out = to(others, others, all_send, all_recv, (dom, partner))
    spread_out.wait_recv()
    spread_out.wait_send()


def gather(images, panels, means, table, pose, group):
    n_rows, n_dom = lax.axis_size("rows"), lax.axis_size("dom")
    rows, pixels = images.shape
    bins, _, order = panels.shape
    chunk = 1280 if pixels % 1280 == 0 else 128
    steps = pixels // chunk
    block = rows // BLOCKS
    ring = 2 * n_dom
    piece = order // (2 * ring)
    swap = pltpu.VMEM((BLOCKS, block // 2, order), F32)
    coeffs, gram = pl.pallas_call(
        functools.partial(gather_kernel, n_rows, n_dom, chunk),
        in_specs=[pl.BlockSpec(memory_space=pl.ANY)] * 4 + [pl.BlockSpec(memory_space=pltpu.VMEM)] * 2,
        out_specs=[pl.BlockSpec(memory_space=pltpu.VMEM)] * 2,
        out_shape=[
            jax.ShapeDtypeStruct((rows, order), F32),
            jax.ShapeDtypeStruct((2 * ring, piece, order), F32),
        ],
        scratch_shapes=[
            pltpu.VMEM(images.shape, BF16),
            pltpu.VMEM(panels.shape, BF16),
            pltpu.VMEM(means.shape, F32),
            pltpu.VMEM(table.shape, F32),
            pltpu.VMEM((rows, 128), BF16),
            pltpu.VMEM((rows, 128), F32),
            pltpu.VMEM((bins, block, order), F32),
            pltpu.VMEM((rows, order), F32),
            swap,
            swap,
            swap,
            pltpu.VMEM((order // 2, order), F32),
            pltpu.VMEM((ring, piece, order), F32),
            pltpu.VMEM((ring, piece, order), F32),
            pltpu.SemaphoreType.DMA((2 + steps * (bins + BLOCKS) + 6 * BLOCKS + 4,)),
        ],
        compiler_params=pltpu.CompilerParams(
            collective_id=0, has_side_effects=True, vmem_limit_bytes=60 * 2**20
        ),
        name="gather",
    )(images, panels, means, table, pose.reshape(1, rows), group.reshape(1, rows))
    return coeffs, gram.reshape(order, order)


def body(images, panels, mean_panels, ctf_table, pose_bin, ctf_group):
    particles = images.shape[0] * lax.axis_size("dom")
    coeffs, gram = gather(images, panels, mean_panels, ctf_table, pose_bin, ctf_group)
    return tuple(finish(gram, coeffs, particles))


def solution(mesh):
    placed = (
        P("dom", "rows"),
        P("dom", "rows", None),
        P("dom", "rows"),
        P(None, "rows"),
        P("dom"),
        P("dom"),
    )
    return jax.shard_map(
        body, mesh=mesh, in_specs=placed, out_specs=(P("dom", None), P()), check_vma=False
    )
```

```python
import functools

import jax
import jax.numpy as jnp
from jax import lax
from jax.experimental import pallas as pl
from jax.experimental.pallas import tpu as pltpu
from jax.sharding import PartitionSpec as P

F32 = jnp.float32
BF16 = jnp.bfloat16


def dot_f32(left, right, dims):
    return lax.dot_general(
        left, right, (dims, ((), ())), precision=lax.Precision.HIGHEST, preferred_element_type=F32
    )


def widen(column, lanes):
    return jnp.concatenate([column] * (lanes // 128), axis=1)


SIZE = 64
PANEL = 16


def factor_block(block):
    lane = lax.broadcasted_iota(jnp.int32, (8, 2 * SIZE), 1)
    sub = lax.broadcasted_iota(jnp.int32, (8, 2 * SIZE), 0)
    tiles = []
    for t in range(SIZE // 8):
        unit = (lane == sub + (8 * t + SIZE)).astype(F32)
        part = jnp.concatenate([block[8 * t : 8 * t + 8], jnp.zeros((8, SIZE), F32)], axis=1)
        tiles.append(part + unit)
    count = len(tiles)
    pivots = [jnp.ones((8, 2 * SIZE), F32) for _ in range(count)]
    for base in range(0, SIZE, PANEL):
        first = base // 8
        cols = [
            [None] * first
            + [jnp.broadcast_to(tiles[t][:, base + j : base + j + 1], (8, 2 * SIZE)) for t in range(first, count)]
            for j in range(PANEL)
        ]
        for j in range(PANEL):
            k = base + j
            row, here = k % 8, k // 8
            pivot = cols[j][here][row : row + 1]
            inverse = 1.0 / pivot
            pivots[here] = jnp.where(sub == row, pivot, pivots[here])
            scale = [None] * count
            for t in range(here, count):
                scale[t] = cols[j][t] * inverse
            scale[here] = jnp.where(sub > row, scale[here], 0.0)
            for later in range(j + 1, PANEL):
                value = cols[later][here][row : row + 1]
                for t in range(here, count):
                    cols[later][t] = cols[later][t] - scale[t] * value
            line = tiles[here][row : row + 1]
            for t in range(here, count):
                tiles[t] = tiles[t] - scale[t] * line
    done = []
    for t in range(count):
        keep = (lane >= SIZE) | (lane >= sub + 8 * t)
        done.append(jnp.where(keep, tiles[t] * lax.rsqrt(pivots[t]), 0.0))
    return jnp.concatenate(done, axis=0)


def finish_kernel(particles, gram, coeffs, scores, factor, work, side):
    order = coeffs.shape[1]
    for h in range(2):
        side_of = slice(h * order // 2, (h + 1) * order // 2)
        work[:, side_of] = gram[:, h].reshape(order, order // 2) * (1.0 / particles)
    spot = lax.broadcasted_iota(jnp.int32, (order, order), 0)
    side[...] = (spot == lax.broadcasted_iota(jnp.int32, (order, order), 1)).astype(F32)
    for start in range(0, order, SIZE):
        stop = start + SIZE
        both = factor_block(work[start:stop, start:stop])
        upper, lower = both[:, :SIZE], both[:, SIZE:]
        if start:
            factor[start:stop, :start] = jnp.zeros((SIZE, start), F32)
        factor[start:stop, start:stop] = upper
        reach = -(-stop // 128) * 128
        row_side = dot_f32(lower, side[start:stop, :reach], ((1,), (0,)))
        side[start:stop, :reach] = row_side
        if stop < order:
            from_col = stop // 128 * 128
            row_work = dot_f32(lower, work[start:stop, from_col:], ((1,), (0,)))
            right = row_work[:, stop - from_col :]
            factor[start:stop, stop:] = right
            work[stop:, from_col:] = work[stop:, from_col:] - dot_f32(right, row_work, ((0,), (0,)))
            side[stop:, :reach] = side[stop:, :reach] - dot_f32(right, row_side, ((0,), (0,)))
    scores[...] = dot_f32(coeffs[...], side[...], ((1,), (1,)))


def finish(gram, coeffs, particles):
    order = coeffs.shape[1]
    return pl.pallas_call(
        functools.partial(finish_kernel, particles),
        in_specs=[pl.BlockSpec(memory_space=pltpu.VMEM)] * 2,
        out_specs=[pl.BlockSpec(memory_space=pltpu.VMEM)] * 2,
        out_shape=[jax.ShapeDtypeStruct(coeffs.shape, F32), jax.ShapeDtypeStruct((order, order), F32)],
        scratch_shapes=[pltpu.VMEM((order, order), F32)] * 2,
        name="finish",
    )(gram, coeffs)


MESH = pl.DeviceIdType.MESH
BLOCKS = 2


def blocks_of(rows):
    first = rows * 4 // 7 // 32 * 32
    return first, rows - first


def gather_kernel(n_rows, n_dom, chunk, images, panels, means, table, pose, group, coeffs, gram, *scratch):
    img, pan, mea, tab, mark, mask, acc, part, near, held, far, wide, give, take, sems = scratch
    row, dom = lax.axis_index("rows"), lax.axis_index("dom")
    side, pair = row % 2, row // 2
    other = 1 - side
    partner = pair * 2 + other
    across = (1 - pair) * 2 + other
    own = (side + pair) % 2
    rows, pixels = images.shape
    bins, groups = panels.shape[0], table.shape[0]
    order = panels.shape[2]
    steps = pixels // chunk
    sizes = blocks_of(rows)
    starts = (0, sizes[0])
    world = n_rows * n_dom
    ring = 2 * n_dom
    spot = dom * 2 + side
    flat = dom * n_rows + row
    piece = order // (2 * ring)
    links = 2 + steps * (bins + BLOCKS)
    pair_send, pair_recv, far_send, far_recv, back_send, back_recv = range(links, links + 6 * BLOCKS, BLOCKS)
    dom_send, dom_recv, all_send, all_recv = range(links + 6 * BLOCKS, links + 6 * BLOCKS + 4)

    def to(source, target, send, recv, place):
        return pltpu.make_async_remote_copy(
            src_ref=source, dst_ref=target, send_sem=sems.at[send], recv_sem=sems.at[recv], device_id=place, device_id_type=MESH
        )

    def local(source, target, sem):
        copy = pltpu.make_async_copy(source, target, sems.at[sem])
        copy.start()
        return copy

    small = [local(table, tab, 0), local(means, mea, 1)]
    weights, pictures = [], [[], []]
    for b in range(BLOCKS):
        for k in range(steps):
            px, at = pl.ds(k * chunk, chunk), pl.ds(starts[b], sizes[b])
            if b == 0:
                weights.append([local(panels.at[w, px], pan.at[w, px], 2 + w * steps + k) for w in range(bins)])
            pictures[b].append(local(images.at[at, px], img.at[at, px], 2 + (bins + b) * steps + k))

    barrier = pltpu.get_barrier_semaphore()

    def greet(step, carry):
        there = (flat + step) % world
        pl.semaphore_signal(
            barrier, inc=1, device_id=(there // n_rows, there % n_rows), device_id_type=MESH
        )
        return carry

    lax.fori_loop(1, world, greet, 0)
    gram[ring:, 0] = jnp.zeros((ring, piece, order // 2), F32)

    mark[...] = jnp.transpose(jnp.broadcast_to(group[...].astype(F32), (128, rows))).astype(jnp.int32)
    mask[...] = jnp.transpose(jnp.broadcast_to(pose[...].astype(F32), (128, rows)))
    for copy in small:
        copy.wait()

    def project(b, k):
        at, px = pl.ds(starts[b], sizes[b]), pl.ds(k * chunk, chunk)
        if b == 0:
            for copy in weights[k]:
                copy.wait()
        pictures[b][k].wait()
        lines = []
        for r in range(starts[b], starts[b] + sizes[b], 8):
            name = widen(mark[r : r + 8, :], chunk)
            line = None
            for base in range(0, groups, 8):
                found = jnp.take_along_axis(tab[base : base + 8, px], name % 8, axis=0, mode="promise_in_bounds")
                line = found if line is None else jnp.where(name >= base, found, line)
            lines.append(line)
        ctf = jnp.concatenate(lines, axis=0)
        second = widen(mask[at, :], chunk) > 0.5
        mean = jnp.where(second, mea[1:2, px], mea[0:1, px])
        weighted = (ctf * (img[at, px].astype(F32) - ctf * mean)).astype(BF16)
        for which in range(2):
            value = jnp.dot(weighted, pan[which, px, :], preferred_element_type=F32)
            if k:
                value = acc[which, : sizes[b], :] + value
            acc[which, : sizes[b], :] = value

    def mine(b, which):
        half = sizes[b] // 2
        return pl.ds(pl.multiple_of(starts[b] + which * half, 8), half)

    first, second, third = [], [], []

    def pair_start(b):
        at, size = pl.ds(starts[b], sizes[b]), sizes[b]
        part[at, :] = jnp.where(widen(mask[at, :], order) > 0.5, acc[1, :size, :], acc[0, :size, :])
        if b == 0:
            pl.semaphore_wait(barrier, world - 1)
        first.append(to(part.at[mine(b, 1 - own)], near.at[mine(b, 0)], pair_send + b, pair_recv + b, (dom, partner)))
        first[b].start()

    def pair_finish(b):
        first[b].wait_recv()
        held[mine(b, 0), :] = part[mine(b, own), :] + near[mine(b, 0), :]
        second.append(to(held.at[mine(b, 0)], far.at[mine(b, 0)], far_send + b, far_recv + b, (dom, across)))
        second[b].start()

    columns = pl.ds(pl.multiple_of(pair * (order // 2), 128), order // 2)

    def square(b):
        second[b].wait_recv()
        coeffs[mine(b, own), :] = held[mine(b, 0), :] + far[mine(b, 0), :]
        ours = coeffs.at[mine(b, own)]
        third.append(to(ours, ours, back_send + b, back_recv + b, (dom, partner)))
        third[b].start()
        return dot_f32(coeffs[mine(b, own), columns], coeffs[mine(b, own), :], ((0,), (0,)))

    for k in range(steps):
        project(0, k)
    pair_start(0)
    for k in range(steps):
        project(1, k)
        if k == min(1, steps - 1):
            pair_finish(0)
    pair_start(1)
    pair_finish(1)
    wide[...] = square(0)
    wide[...] += square(1)
    left = order // 2
    for j in range(ring):
        give[j, 0] = wide[j * piece : (j + 1) * piece, :left]
        give[j, 1] = wide[j * piece : (j + 1) * piece, left:]
    index = pair * ring + spot

    def part_of(ref, place, upper):
        return ref.at[place] if upper else ref.at[place, 1]

    def deal(step, upper):
        there = (spot + step) % ring
        place = (there // 2, pair * 2 + there % 2)
        return to(part_of(give, there, upper), part_of(take, spot, upper), dom_send, dom_recv, place)

    def spread(step, upper):
        there = (flat + step) % world
        ours = part_of(gram, index, upper)
        return to(ours, ours, all_send, all_recv + (0 if upper else 1), (there // n_rows, there % n_rows))

    def each(count, action):
        def one(step, carry):
            action(step)
            return carry

        lax.fori_loop(1, count, one, 0)

    def many(ref, count, upper, send, recv):
        those = part_of(ref, pl.ds(0, count), upper)
        return to(those, those, send, recv, (dom, partner))

    def exchange(upper):
        each(ring, lambda step: deal(step, upper).start())
        take[spot] = give[spot]
        dealt = many(take, ring - 1, upper, dom_send, dom_recv)
        dealt.wait_recv()
        for h in range(0 if upper else 1, 2):
            total = take[0, h]
            for j in range(1, ring):
                total = total + take[j, h]
            gram[index, h] = total
        each(world, lambda step: spread(step, upper).start())
        dealt.wait_send()
        many(gram, ring - 1 if upper else ring, True, all_send, all_recv).wait_recv()
        many(gram, ring if upper else ring - 1, False, all_send, all_recv + 1).wait_recv()
        many(gram, world - 1, upper, all_send, all_recv).wait_send()

    @pl.when(pair == 0)
    def _():
        exchange(True)

    @pl.when(pair == 1)
    def _():
        exchange(False)

    for copy in third:
        copy.wait_recv()
    for copy in first + second + third:
        copy.wait_send()


def gather(images, panels, means, table, pose, group):
    n_rows, n_dom = lax.axis_size("rows"), lax.axis_size("dom")
    rows, pixels = images.shape
    bins, _, order = panels.shape
    chunk = 1280 if pixels % 1280 == 0 else 128
    steps = pixels // chunk
    block = blocks_of(rows)[0]
    ring = 2 * n_dom
    piece = order // (2 * ring)
    swap = pltpu.VMEM((rows, order), F32)
    coeffs, gram = pl.pallas_call(
        functools.partial(gather_kernel, n_rows, n_dom, chunk),
        in_specs=[pl.BlockSpec(memory_space=pl.ANY)] * 4 + [pl.BlockSpec(memory_space=pltpu.VMEM)] * 2,
        out_specs=[pl.BlockSpec(memory_space=pltpu.VMEM)] * 2,
        out_shape=[
            jax.ShapeDtypeStruct((rows, order), F32),
            jax.ShapeDtypeStruct((2 * ring, 2, piece, order // 2), F32),
        ],
        scratch_shapes=[
            pltpu.VMEM(images.shape, BF16),
            pltpu.VMEM(panels.shape, BF16),
            pltpu.VMEM(means.shape, F32),
            pltpu.VMEM(table.shape, F32),
            pltpu.VMEM((rows, 128), jnp.int32),
            pltpu.VMEM((rows, 128), F32),
            pltpu.VMEM((bins, block, order), F32),
            pltpu.VMEM((rows, order), F32),
            swap,
            swap,
            swap,
            pltpu.VMEM((order // 2, order), F32),
            pltpu.VMEM((ring, 2, piece, order // 2), F32),
            pltpu.VMEM((ring, 2, piece, order // 2), F32),
            pltpu.SemaphoreType.DMA((2 + steps * (bins + BLOCKS) + 6 * BLOCKS + 5,)),
        ],
        compiler_params=pltpu.CompilerParams(
            collective_id=0, has_side_effects=True, vmem_limit_bytes=60 * 2**20
        ),
        name="gather",
    )(images, panels, means, table, pose.reshape(1, rows), group.reshape(1, rows))
    return coeffs, gram


def body(images, panels, mean_panels, ctf_table, pose_bin, ctf_group):
    particles = images.shape[0] * lax.axis_size("dom")
    coeffs, gram = gather(images, panels, mean_panels, ctf_table, pose_bin, ctf_group)
    return tuple(finish(gram, coeffs, particles))


def solution(mesh):
    placed = (
        P("dom", "rows"),
        P("dom", "rows", None),
        P("dom", "rows"),
        P(None, "rows"),
        P("dom"),
        P("dom"),
    )
    return jax.shard_map(
        body, mesh=mesh, in_specs=placed, out_specs=(P("dom", None), P()), check_vma=False
    )
```

```python
import functools

import jax
import jax.numpy as jnp
from jax import lax
from jax.experimental import pallas as pl
from jax.experimental.pallas import tpu as pltpu
from jax.sharding import PartitionSpec as P

F32 = jnp.float32
BF16 = jnp.bfloat16


def dot_f32(left, right, dims):
    return lax.dot_general(
        left, right, (dims, ((), ())), precision=lax.Precision.HIGHEST, preferred_element_type=F32
    )


def widen(column, lanes):
    return jnp.concatenate([column] * (lanes // 128), axis=1)


SIZE = 64
PANEL = 16


def factor_block(block):
    lane = lax.broadcasted_iota(jnp.int32, (8, 2 * SIZE), 1)
    sub = lax.broadcasted_iota(jnp.int32, (8, 2 * SIZE), 0)
    tiles = []
    for t in range(SIZE // 8):
        unit = (lane == sub + (8 * t + SIZE)).astype(F32)
        part = jnp.concatenate([block[8 * t : 8 * t + 8], jnp.zeros((8, SIZE), F32)], axis=1)
        tiles.append(part + unit)
    count = len(tiles)
    pivots = [jnp.ones((8, 2 * SIZE), F32) for _ in range(count)]
    for base in range(0, SIZE, PANEL):
        first = base // 8
        cols = [
            [None] * first
            + [jnp.broadcast_to(tiles[t][:, base + j : base + j + 1], (8, 2 * SIZE)) for t in range(first, count)]
            for j in range(PANEL)
        ]
        for j in range(PANEL):
            k = base + j
            row, here = k % 8, k // 8
            pivot = cols[j][here][row : row + 1]
            inverse = 1.0 / pivot
            pivots[here] = jnp.where(sub == row, pivot, pivots[here])
            scale = [None] * count
            for t in range(here, count):
                scale[t] = cols[j][t] * inverse
            scale[here] = jnp.where(sub > row, scale[here], 0.0)
            for later in range(j + 1, PANEL):
                value = cols[later][here][row : row + 1]
                for t in range(here, count):
                    cols[later][t] = cols[later][t] - scale[t] * value
            line = tiles[here][row : row + 1]
            for t in range(here, count):
                tiles[t] = tiles[t] - scale[t] * line
    done = []
    for t in range(count):
        keep = (lane >= SIZE) | (lane >= sub + 8 * t)
        done.append(jnp.where(keep, tiles[t] * lax.rsqrt(pivots[t]), 0.0))
    return jnp.concatenate(done, axis=0)


def halves(value):
    high = value.astype(BF16)
    return high, (value - high.astype(F32)).astype(BF16)


def dot_split(left, right, dims):
    (a, b), (c, d) = left, right

    def one(x, y):
        return lax.dot_general(x, y, (dims, ((), ())), preferred_element_type=F32)

    return one(a, c) + (one(a, d) + one(b, c))


def dot_rows(left, right):
    (a, b), (c, d) = left, right
    tall = jnp.concatenate([a, a, b], axis=0)
    other = jnp.concatenate([c, d, c], axis=0)
    return lax.dot_general(tall, other, (((0,), (0,)), ((), ())), preferred_element_type=F32)


def lanes(pair, start, stop):
    return tuple(part[:, start:stop] for part in pair)


def finish_kernel(particles, gram, coeffs, scores, factor, work, side, high, low):
    order = coeffs.shape[1]
    middle = order // 2
    for h in range(2):
        work[:, h * middle : (h + 1) * middle] = gram[:, h].reshape(order, middle) * (1.0 / particles)
    spot = lax.broadcasted_iota(jnp.int32, (order, order), 0)
    side[...] = (spot == lax.broadcasted_iota(jnp.int32, (order, order), 1)).astype(F32)
    high[...], low[...] = halves(coeffs[...])

    for start in range(0, order, SIZE):
        stop = start + SIZE
        both = factor_block(work[start:stop, start:stop])
        upper, lower = both[:, :SIZE], halves(both[:, SIZE:])
        if start:
            factor[start:stop, :start] = jnp.zeros((SIZE, start), F32)
        factor[start:stop, start:stop] = upper
        reach = -(-stop // 128) * 128
        base = stop // 128 * 128
        if stop < order:
            row_work = dot_split(lower, halves(work[start:stop, base:]), ((1,), (0,)))
            factor[start:stop, stop:] = row_work[:, stop - base :]
            cut = halves(row_work)
            near = lanes(cut, 0, 128)
            work[stop : base + 128, base:] = work[stop : base + 128, base:] - dot_rows(near, cut)[stop - base :]
        row_side = dot_split(lower, halves(side[start:stop, :reach]), ((1,), (0,)))
        side[start:stop, :reach] = row_side
        if stop < order:
            aside = halves(row_side)
            side[stop : base + 128, :reach] = side[stop : base + 128, :reach] - dot_rows(near, aside)[stop - base :]
            if base + 128 < order:
                rest = lanes(cut, 128, order - base)
                work[base + 128 :, base + 128 :] = work[base + 128 :, base + 128 :] - dot_rows(rest, rest)
                side[base + 128 :, :reach] = side[base + 128 :, :reach] - dot_rows(rest, aside)
        if stop % 128 == 0:
            columns = slice(stop - 128, stop)
            scores[:, columns] = dot_split(
                (high[:, :stop], low[:, :stop]), halves(side[columns, :stop]), ((1,), (1,))
            )


def finish(gram, coeffs, particles):
    order = coeffs.shape[1]
    return pl.pallas_call(
        functools.partial(finish_kernel, particles),
        in_specs=[pl.BlockSpec(memory_space=pltpu.VMEM)] * 2,
        out_specs=[pl.BlockSpec(memory_space=pltpu.VMEM)] * 2,
        out_shape=[jax.ShapeDtypeStruct(coeffs.shape, F32), jax.ShapeDtypeStruct((order, order), F32)],
        scratch_shapes=[pltpu.VMEM((order, order), F32)] * 2 + [pltpu.VMEM(coeffs.shape, BF16)] * 2,
        name="finish",
    )(gram, coeffs)


MESH = pl.DeviceIdType.MESH
BLOCKS = 2


def blocks_of(rows):
    first = rows * 4 // 7 // 32 * 32
    return first, rows - first


def gather_kernel(n_rows, n_dom, chunk, images, panels, means, table, pose, group, coeffs, gram, *scratch):
    img, pan, mea, tab, mark, mask, acc, part, near, held, far, wide, give, take, sems = scratch
    row, dom = lax.axis_index("rows"), lax.axis_index("dom")
    side, pair = row % 2, row // 2
    other = 1 - side
    partner = pair * 2 + other
    across = (1 - pair) * 2 + other
    own = (side + pair) % 2
    rows, pixels = images.shape
    bins, groups = panels.shape[0], table.shape[0]
    order = panels.shape[2]
    steps = pixels // chunk
    sizes = blocks_of(rows)
    starts = (0, sizes[0])
    world = n_rows * n_dom
    ring = 2 * n_dom
    spot = dom * 2 + side
    flat = dom * n_rows + row
    piece = order // (2 * ring)
    links = 2 + steps * (bins + BLOCKS)
    pair_send, pair_recv, far_send, far_recv, back_send, back_recv = range(links, links + 6 * BLOCKS, BLOCKS)
    dom_send, dom_recv, all_send, all_recv = range(links + 6 * BLOCKS, links + 6 * BLOCKS + 4)

    def to(source, target, send, recv, place):
        return pltpu.make_async_remote_copy(
            src_ref=source, dst_ref=target, send_sem=sems.at[send], recv_sem=sems.at[recv], device_id=place, device_id_type=MESH
        )

    def local(source, target, sem):
        copy = pltpu.make_async_copy(source, target, sems.at[sem])
        copy.start()
        return copy

    small = [local(table, tab, 0), local(means, mea, 1)]
    weights, pictures = [], [[], []]
    for b in range(BLOCKS):
        for k in range(steps):
            px, at = pl.ds(k * chunk, chunk), pl.ds(starts[b], sizes[b])
            if b == 0:
                weights.append([local(panels.at[w, px], pan.at[w, px], 2 + w * steps + k) for w in range(bins)])
            pictures[b].append(local(images.at[at, px], img.at[at, px], 2 + (bins + b) * steps + k))

    barrier = pltpu.get_barrier_semaphore()

    def greet(step, carry):
        there = (flat + step) % world
        pl.semaphore_signal(
            barrier, inc=1, device_id=(there // n_rows, there % n_rows), device_id_type=MESH
        )
        return carry

    lax.fori_loop(1, world, greet, 0)
    gram[ring:, 0] = jnp.zeros((ring, piece, order // 2), F32)

    mark[...] = jnp.transpose(jnp.broadcast_to(group[...].astype(F32), (128, rows))).astype(jnp.int32)
    mask[...] = jnp.transpose(jnp.broadcast_to(pose[...].astype(F32), (128, rows)))
    for copy in small:
        copy.wait()

    def project(b, k):
        at, px = pl.ds(starts[b], sizes[b]), pl.ds(k * chunk, chunk)
        if b == 0:
            for copy in weights[k]:
                copy.wait()
        pictures[b][k].wait()
        lines = []
        for r in range(starts[b], starts[b] + sizes[b], 8):
            name = widen(mark[r : r + 8, :], chunk)
            line = None
            for base in range(0, groups, 8):
                found = jnp.take_along_axis(tab[base : base + 8, px], name % 8, axis=0, mode="promise_in_bounds")
                line = found if line is None else jnp.where(name >= base, found, line)
            lines.append(line)
        ctf = jnp.concatenate(lines, axis=0)
        second = widen(mask[at, :], chunk) > 0.5
        mean = jnp.where(second, mea[1:2, px], mea[0:1, px])
        weighted = (ctf * (img[at, px].astype(F32) - ctf * mean)).astype(BF16)
        for which in range(2):
            value = jnp.dot(weighted, pan[which, px, :], preferred_element_type=F32)
            if k:
                value = acc[which, : sizes[b], :] + value
            acc[which, : sizes[b], :] = value

    def mine(b, which):
        half = sizes[b] // 2
        return pl.ds(pl.multiple_of(starts[b] + which * half, 8), half)

    first, second, third = [], [], []

    def pair_start(b):
        at, size = pl.ds(starts[b], sizes[b]), sizes[b]
        part[at, :] = jnp.where(widen(mask[at, :], order) > 0.5, acc[1, :size, :], acc[0, :size, :])
        if b == 0:
            pl.semaphore_wait(barrier, world - 1)
        first.append(to(part.at[mine(b, 1 - own)], near.at[mine(b, 0)], pair_send + b, pair_recv + b, (dom, partner)))
        first[b].start()

    def pair_finish(b):
        first[b].wait_recv()
        held[mine(b, 0), :] = part[mine(b, own), :] + near[mine(b, 0), :]
        second.append(to(held.at[mine(b, 0)], far.at[mine(b, 0)], far_send + b, far_recv + b, (dom, across)))
        second[b].start()

    columns = pl.ds(pl.multiple_of(pair * (order // 2), 128), order // 2)

    def square(b):
        second[b].wait_recv()
        coeffs[mine(b, own), :] = held[mine(b, 0), :] + far[mine(b, 0), :]
        ours = coeffs.at[mine(b, own)]
        third.append(to(ours, ours, back_send + b, back_recv + b, (dom, partner)))
        third[b].start()
        return dot_f32(coeffs[mine(b, own), columns], coeffs[mine(b, own), :], ((0,), (0,)))

    for k in range(steps):
        project(0, k)
    pair_start(0)
    for k in range(steps):
        project(1, k)
        if k == min(1, steps - 1):
            pair_finish(0)
    pair_start(1)
    pair_finish(1)
    wide[...] = square(0)
    wide[...] += square(1)
    left = order // 2
    for j in range(ring):
        give[j, 0] = wide[j * piece : (j + 1) * piece, :left]
        give[j, 1] = wide[j * piece : (j + 1) * piece, left:]
    index = pair * ring + spot

    def part_of(ref, place, upper):
        return ref.at[place] if upper else ref.at[place, 1]

    def deal(step, upper):
        there = (spot + step) % ring
        place = (there // 2, pair * 2 + there % 2)
        return to(part_of(give, there, upper), part_of(take, spot, upper), dom_send, dom_recv, place)

    def spread(step, upper):
        there = (flat + step) % world
        ours = part_of(gram, index, upper)
        return to(ours, ours, all_send, all_recv + (0 if upper else 1), (there // n_rows, there % n_rows))

    def each(count, action):
        def one(step, carry):
            action(step)
            return carry

        lax.fori_loop(1, count, one, 0)

    def many(ref, count, upper, send, recv):
        those = part_of(ref, pl.ds(0, count), upper)
        return to(those, those, send, recv, (dom, partner))

    def exchange(upper):
        each(ring, lambda step: deal(step, upper).start())
        take[spot] = give[spot]
        dealt = many(take, ring - 1, upper, dom_send, dom_recv)
        dealt.wait_recv()
        for h in range(0 if upper else 1, 2):
            total = take[0, h]
            for j in range(1, ring):
                total = total + take[j, h]
            gram[index, h] = total
        each(world, lambda step: spread(step, upper).start())
        dealt.wait_send()
        many(gram, ring - 1 if upper else ring, True, all_send, all_recv).wait_recv()
        many(gram, ring if upper else ring - 1, False, all_send, all_recv + 1).wait_recv()
        many(gram, world - 1, upper, all_send, all_recv).wait_send()

    @pl.when(pair == 0)
    def _():
        exchange(True)

    @pl.when(pair == 1)
    def _():
        exchange(False)

    for copy in third:
        copy.wait_recv()
    for copy in first + second + third:
        copy.wait_send()


def gather(images, panels, means, table, pose, group):
    n_rows, n_dom = lax.axis_size("rows"), lax.axis_size("dom")
    rows, pixels = images.shape
    bins, _, order = panels.shape
    chunk = 1280 if pixels % 1280 == 0 else 128
    steps = pixels // chunk
    block = blocks_of(rows)[0]
    ring = 2 * n_dom
    piece = order // (2 * ring)
    swap = pltpu.VMEM((rows, order), F32)
    coeffs, gram = pl.pallas_call(
        functools.partial(gather_kernel, n_rows, n_dom, chunk),
        in_specs=[pl.BlockSpec(memory_space=pltpu.HBM)] * 4 + [pl.BlockSpec(memory_space=pltpu.VMEM)] * 2,
        out_specs=[pl.BlockSpec(memory_space=pltpu.VMEM)] * 2,
        out_shape=[
            pltpu.VMEM((rows, order), F32),
            pltpu.VMEM((2 * ring, 2, piece, order // 2), F32),
        ],
        scratch_shapes=[
            pltpu.VMEM(images.shape, BF16),
            pltpu.VMEM(panels.shape, BF16),
            pltpu.VMEM(means.shape, F32),
            pltpu.VMEM(table.shape, F32),
            pltpu.VMEM((rows, 128), jnp.int32),
            pltpu.VMEM((rows, 128), F32),
            pltpu.VMEM((bins, block, order), F32),
            pltpu.VMEM((rows, order), F32),
            swap,
            swap,
            swap,
            pltpu.VMEM((order // 2, order), F32),
            pltpu.VMEM((ring, 2, piece, order // 2), F32),
            pltpu.VMEM((ring, 2, piece, order // 2), F32),
            pltpu.SemaphoreType.DMA((2 + steps * (bins + BLOCKS) + 6 * BLOCKS + 5,)),
        ],
        compiler_params=pltpu.CompilerParams(
            collective_id=0, has_side_effects=True, vmem_limit_bytes=60 * 2**20
        ),
        name="gather",
    )(images, panels, means, table, pose.reshape(1, rows), group.reshape(1, rows))
    return coeffs, gram


def body(images, panels, mean_panels, ctf_table, pose_bin, ctf_group):
    particles = images.shape[0] * lax.axis_size("dom")
    coeffs, gram = gather(images, panels, mean_panels, ctf_table, pose_bin, ctf_group)
    return tuple(finish(pltpu.with_memory_space_constraint(gram, pltpu.VMEM), pltpu.with_memory_space_constraint(coeffs, pltpu.VMEM), particles))


def solution(mesh):
    placed = (
        P("dom", "rows"),
        P("dom", "rows", None),
        P("dom", "rows"),
        P(None, "rows"),
        P("dom"),
        P("dom"),
    )
    return jax.shard_map(
        body, mesh=mesh, in_specs=placed, out_specs=(P("dom", None), P()), check_vma=False
    )
```

```python
import functools

import jax
import jax.numpy as jnp
from jax import lax
from jax.experimental import pallas as pl
from jax.experimental.pallas import tpu as pltpu
from jax.sharding import PartitionSpec as P

F32 = jnp.float32
BF16 = jnp.bfloat16


def dot_f32(left, right, dims):
    return lax.dot_general(
        left, right, (dims, ((), ())), precision=lax.Precision.HIGHEST, preferred_element_type=F32
    )


def widen(column, lanes):
    return jnp.concatenate([column] * (lanes // 128), axis=1)


SIZE = 64
PANEL = 16


def factor_block(block):
    lane = lax.broadcasted_iota(jnp.int32, (8, 2 * SIZE), 1)
    sub = lax.broadcasted_iota(jnp.int32, (8, 2 * SIZE), 0)
    tiles = []
    for t in range(SIZE // 8):
        unit = (lane == sub + (8 * t + SIZE)).astype(F32)
        part = jnp.concatenate([block[8 * t : 8 * t + 8], jnp.zeros((8, SIZE), F32)], axis=1)
        tiles.append(part + unit)
    count = len(tiles)
    pivots = [jnp.ones((8, 2 * SIZE), F32) for _ in range(count)]
    for base in range(0, SIZE, PANEL):
        first = base // 8
        cols = [
            [None] * first
            + [jnp.broadcast_to(tiles[t][:, base + j : base + j + 1], (8, 2 * SIZE)) for t in range(first, count)]
            for j in range(PANEL)
        ]
        for j in range(PANEL):
            k = base + j
            row, here = k % 8, k // 8
            pivot = cols[j][here][row : row + 1]
            inverse = 1.0 / pivot
            pivots[here] = jnp.where(sub == row, pivot, pivots[here])
            scale = [None] * count
            for t in range(here, count):
                scale[t] = cols[j][t] * inverse
            scale[here] = jnp.where(sub > row, scale[here], 0.0)
            for later in range(j + 1, PANEL):
                value = cols[later][here][row : row + 1]
                for t in range(here, count):
                    cols[later][t] = cols[later][t] - scale[t] * value
            line = tiles[here][row : row + 1]
            for t in range(here, count):
                tiles[t] = tiles[t] - scale[t] * line
    done = []
    for t in range(count):
        keep = (lane >= SIZE) | (lane >= sub + 8 * t)
        done.append(jnp.where(keep, tiles[t] * lax.rsqrt(pivots[t]), 0.0))
    return jnp.concatenate(done, axis=0)


def halves(value):
    high = value.astype(BF16)
    return high, (value - high.astype(F32)).astype(BF16)


def dot_split(left, right, dims):
    (a, b), (c, d) = left, right

    def one(x, y):
        return lax.dot_general(x, y, (dims, ((), ())), preferred_element_type=F32)

    return one(a, c) + (one(a, d) + one(b, c))


def dot_rows(left, right):
    (a, b), (c, d) = left, right
    tall = jnp.concatenate([a, a, b], axis=0)
    other = jnp.concatenate([c, d, c], axis=0)
    return lax.dot_general(tall, other, (((0,), (0,)), ((), ())), preferred_element_type=F32)


def lanes(pair, start, stop):
    return tuple(part[:, start:stop] for part in pair)


def finish_kernel(particles, gram, coeffs, scores, factor, work, side, high, low):
    order = coeffs.shape[1]
    middle = order // 2
    for h in range(2):
        work[:, h * middle : (h + 1) * middle] = gram[:, h].reshape(order, middle) * (1.0 / particles)
    spot = lax.broadcasted_iota(jnp.int32, (order, order), 0)
    side[...] = (spot == lax.broadcasted_iota(jnp.int32, (order, order), 1)).astype(F32)
    high[...], low[...] = halves(coeffs[...])

    for start in range(0, order, SIZE):
        stop = start + SIZE
        both = factor_block(work[start:stop, start:stop])
        upper, lower = both[:, :SIZE], halves(both[:, SIZE:])
        if start:
            factor[start:stop, :start] = jnp.zeros((SIZE, start), F32)
        factor[start:stop, start:stop] = upper
        reach = -(-stop // 128) * 128
        base = stop // 128 * 128
        if stop < order:
            row_work = dot_split(lower, halves(work[start:stop, base:]), ((1,), (0,)))
            factor[start:stop, stop:] = row_work[:, stop - base :]
            cut = halves(row_work)
            near = lanes(cut, 0, 128)
            work[stop : base + 128, base:] = work[stop : base + 128, base:] - dot_rows(near, cut)[stop - base :]
        row_side = dot_split(lower, halves(side[start:stop, :reach]), ((1,), (0,)))
        side[start:stop, :reach] = row_side
        if stop < order:
            aside = halves(row_side)
            side[stop : base + 128, :reach] = side[stop : base + 128, :reach] - dot_rows(near, aside)[stop - base :]
            if base + 128 < order:
                rest = lanes(cut, 128, order - base)
                work[base + 128 :, base + 128 :] = work[base + 128 :, base + 128 :] - dot_rows(rest, rest)
                side[base + 128 :, :reach] = side[base + 128 :, :reach] - dot_rows(rest, aside)
        if stop % 128 == 0:
            columns = slice(stop - 128, stop)
            scores[:, columns] = dot_split(
                (high[:, :stop], low[:, :stop]), halves(side[columns, :stop]), ((1,), (1,))
            )


def finish(gram, coeffs, particles):
    order = coeffs.shape[1]
    return pl.pallas_call(
        functools.partial(finish_kernel, particles),
        in_specs=[pl.BlockSpec(memory_space=pltpu.VMEM)] * 2,
        out_specs=[pl.BlockSpec(memory_space=pltpu.VMEM)] * 2,
        out_shape=[jax.ShapeDtypeStruct(coeffs.shape, F32), jax.ShapeDtypeStruct((order, order), F32)],
        scratch_shapes=[pltpu.VMEM((order, order), F32)] * 2 + [pltpu.VMEM(coeffs.shape, BF16)] * 2,
        name="finish",
    )(gram, coeffs)


MESH = pl.DeviceIdType.MESH
BLOCKS = 3


def blocks_of(rows):
    first, second = rows * 5 // 14 // 32 * 32, rows * 5 // 14 // 32 * 32
    return first, second, rows - first - second


def gather_kernel(n_rows, n_dom, chunk, images, panels, means, table, pose, group, coeffs, gram, *scratch):
    img, pan, mea, tab, mark, mask, acc, part, near, held, far, wide, give, take, sems = scratch
    row, dom = lax.axis_index("rows"), lax.axis_index("dom")
    side, pair = row % 2, row // 2
    other = 1 - side
    partner = pair * 2 + other
    across = (1 - pair) * 2 + other
    own = (side + pair) % 2
    rows, pixels = images.shape
    bins, groups = panels.shape[0], table.shape[0]
    order = panels.shape[2]
    steps = pixels // chunk
    sizes = blocks_of(rows)
    starts = (0, sizes[0], sizes[0] + sizes[1])
    world = n_rows * n_dom
    ring = 2 * n_dom
    spot = dom * 2 + side
    flat = dom * n_rows + row
    piece = order // (2 * ring)
    links = 2 + steps * (bins + BLOCKS)
    pair_send, pair_recv, far_send, far_recv, back_send, back_recv = range(links, links + 6 * BLOCKS, BLOCKS)
    dom_send, dom_recv, all_send, all_recv = range(links + 6 * BLOCKS, links + 6 * BLOCKS + 4)

    def to(source, target, send, recv, place):
        return pltpu.make_async_remote_copy(
            src_ref=source, dst_ref=target, send_sem=sems.at[send], recv_sem=sems.at[recv], device_id=place, device_id_type=MESH
        )

    def local(source, target, sem):
        copy = pltpu.make_async_copy(source, target, sems.at[sem])
        copy.start()
        return copy

    small = [local(table, tab, 0), local(means, mea, 1)]
    weights, pictures = [], [[] for _ in range(BLOCKS)]
    for b in range(BLOCKS):
        for k in range(steps):
            px, at = pl.ds(k * chunk, chunk), pl.ds(starts[b], sizes[b])
            if b == 0:
                weights.append([local(panels.at[w, px], pan.at[w, px], 2 + w * steps + k) for w in range(bins)])
            pictures[b].append(local(images.at[at, px], img.at[at, px], 2 + (bins + b) * steps + k))

    barrier = pltpu.get_barrier_semaphore()

    def greet(step, carry):
        there = (flat + step) % world
        pl.semaphore_signal(
            barrier, inc=1, device_id=(there // n_rows, there % n_rows), device_id_type=MESH
        )
        return carry

    lax.fori_loop(1, world, greet, 0)
    gram[ring:, 0] = jnp.zeros((ring, piece, order // 2), F32)

    mark[...] = jnp.transpose(jnp.broadcast_to(group[...].astype(F32), (128, rows))).astype(jnp.int32)
    mask[...] = jnp.transpose(jnp.broadcast_to(pose[...].astype(F32), (128, rows)))
    for copy in small:
        copy.wait()

    def project(b, k):
        at, px = pl.ds(starts[b], sizes[b]), pl.ds(k * chunk, chunk)
        if b == 0:
            for copy in weights[k]:
                copy.wait()
        pictures[b][k].wait()
        lines = []
        for r in range(starts[b], starts[b] + sizes[b], 8):
            name = widen(mark[r : r + 8, :], chunk)
            line = None
            for base in range(0, groups, 8):
                found = jnp.take_along_axis(tab[base : base + 8, px], name % 8, axis=0, mode="promise_in_bounds")
                line = found if line is None else jnp.where(name >= base, found, line)
            lines.append(line)
        ctf = jnp.concatenate(lines, axis=0)
        second = widen(mask[at, :], chunk) > 0.5
        mean = jnp.where(second, mea[1:2, px], mea[0:1, px])
        weighted = (ctf * (img[at, px].astype(F32) - ctf * mean)).astype(BF16)
        for which in range(2):
            value = jnp.dot(weighted, pan[which, px, :], preferred_element_type=F32)
            if k:
                value = acc[which, : sizes[b], :] + value
            acc[which, : sizes[b], :] = value

    def mine(b, which):
        half = sizes[b] // 2
        return pl.ds(pl.multiple_of(starts[b] + which * half, 8), half)

    first, second, third = [], [], []

    def pair_start(b):
        at, size = pl.ds(starts[b], sizes[b]), sizes[b]
        part[at, :] = jnp.where(widen(mask[at, :], order) > 0.5, acc[1, :size, :], acc[0, :size, :])
        if b == 0:
            pl.semaphore_wait(barrier, world - 1)
        first.append(to(part.at[mine(b, 1 - own)], near.at[mine(b, 0)], pair_send + b, pair_recv + b, (dom, partner)))
        first[b].start()

    def pair_finish(b):
        first[b].wait_recv()
        held[mine(b, 0), :] = part[mine(b, own), :] + near[mine(b, 0), :]
        second.append(to(held.at[mine(b, 0)], far.at[mine(b, 0)], far_send + b, far_recv + b, (dom, across)))
        second[b].start()

    columns = pl.ds(pl.multiple_of(pair * (order // 2), 128), order // 2)

    def square(b):
        second[b].wait_recv()
        coeffs[mine(b, own), :] = held[mine(b, 0), :] + far[mine(b, 0), :]
        ours = coeffs.at[mine(b, own)]
        third.append(to(ours, ours, back_send + b, back_recv + b, (dom, partner)))
        third[b].start()
        return dot_rows(halves(coeffs[mine(b, own), columns]), halves(coeffs[mine(b, own), :]))

    for b in range(BLOCKS):
        for k in range(steps):
            project(b, k)
            if b and k == min(2, steps - 1):
                pair_finish(b - 1)
        pair_start(b)
    pair_finish(BLOCKS - 1)
    wide[...] = square(0)
    for b in range(1, BLOCKS):
        wide[...] += square(b)
    left = order // 2
    for j in range(ring):
        give[j, 0] = wide[j * piece : (j + 1) * piece, :left]
        give[j, 1] = wide[j * piece : (j + 1) * piece, left:]
    index = pair * ring + spot

    def part_of(ref, place, upper):
        return ref.at[place] if upper else ref.at[place, 1]

    def deal(step, upper):
        there = (spot + step) % ring
        place = (there // 2, pair * 2 + there % 2)
        return to(part_of(give, there, upper), part_of(take, spot, upper), dom_send, dom_recv, place)

    def spread(step, upper):
        there = (flat + step) % world
        ours = part_of(gram, index, upper)
        return to(ours, ours, all_send, all_recv + (0 if upper else 1), (there // n_rows, there % n_rows))

    def each(count, action):
        def one(step, carry):
            action(step)
            return carry

        lax.fori_loop(1, count, one, 0)

    def many(ref, count, upper, send, recv):
        those = part_of(ref, pl.ds(0, count), upper)
        return to(those, those, send, recv, (dom, partner))

    def exchange(upper):
        each(ring, lambda step: deal(step, upper).start())
        take[spot] = give[spot]
        dealt = many(take, ring - 1, upper, dom_send, dom_recv)
        dealt.wait_recv()
        for h in range(0 if upper else 1, 2):
            total = take[0, h]
            for j in range(1, ring):
                total = total + take[j, h]
            gram[index, h] = total
        each(world, lambda step: spread(step, upper).start())
        dealt.wait_send()
        many(gram, ring - 1 if upper else ring, True, all_send, all_recv).wait_recv()
        many(gram, ring if upper else ring - 1, False, all_send, all_recv + 1).wait_recv()
        many(gram, world - 1, upper, all_send, all_recv).wait_send()

    @pl.when(pair == 0)
    def _():
        exchange(True)

    @pl.when(pair == 1)
    def _():
        exchange(False)

    for copy in third:
        copy.wait_recv()
    for copy in first + second + third:
        copy.wait_send()


def gather(images, panels, means, table, pose, group):
    n_rows, n_dom = lax.axis_size("rows"), lax.axis_size("dom")
    rows, pixels = images.shape
    bins, _, order = panels.shape
    chunk = 1280 if pixels % 1280 == 0 else 128
    steps = pixels // chunk
    block = max(blocks_of(rows))
    ring = 2 * n_dom
    piece = order // (2 * ring)
    swap = pltpu.VMEM((rows, order), F32)
    coeffs, gram = pl.pallas_call(
        functools.partial(gather_kernel, n_rows, n_dom, chunk),
        in_specs=[pl.BlockSpec(memory_space=pltpu.HBM)] * 4 + [pl.BlockSpec(memory_space=pltpu.VMEM)] * 2,
        out_specs=[pl.BlockSpec(memory_space=pltpu.VMEM)] * 2,
        out_shape=[
            pltpu.VMEM((rows, order), F32),
            pltpu.VMEM((2 * ring, 2, piece, order // 2), F32),
        ],
        scratch_shapes=[
            pltpu.VMEM(images.shape, BF16),
            pltpu.VMEM(panels.shape, BF16),
            pltpu.VMEM(means.shape, F32),
            pltpu.VMEM(table.shape, F32),
            pltpu.VMEM((rows, 128), jnp.int32),
            pltpu.VMEM((rows, 128), F32),
            pltpu.VMEM((bins, block, order), F32),
            pltpu.VMEM((rows, order), F32),
            swap,
            swap,
            swap,
            pltpu.VMEM((order // 2, order), F32),
            pltpu.VMEM((ring, 2, piece, order // 2), F32),
            pltpu.VMEM((ring, 2, piece, order // 2), F32),
            pltpu.SemaphoreType.DMA((2 + steps * (bins + BLOCKS) + 6 * BLOCKS + 5,)),
        ],
        compiler_params=pltpu.CompilerParams(
            collective_id=0, has_side_effects=True, vmem_limit_bytes=60 * 2**20
        ),
        name="gather",
    )(images, panels, means, table, pose.reshape(1, rows), group.reshape(1, rows))
    return coeffs, gram


def body(images, panels, mean_panels, ctf_table, pose_bin, ctf_group):
    particles = images.shape[0] * lax.axis_size("dom")
    coeffs, gram = gather(images, panels, mean_panels, ctf_table, pose_bin, ctf_group)
    return tuple(finish(pltpu.with_memory_space_constraint(gram, pltpu.VMEM), pltpu.with_memory_space_constraint(coeffs, pltpu.VMEM), particles))


def solution(mesh):
    placed = (
        P("dom", "rows"),
        P("dom", "rows", None),
        P("dom", "rows"),
        P(None, "rows"),
        P("dom"),
        P("dom"),
    )
    return jax.shard_map(
        body, mesh=mesh, in_specs=placed, out_specs=(P("dom", None), P()), check_vma=False
    )
```

```python
import functools

import jax
import jax.numpy as jnp
from jax import lax
from jax.experimental import pallas as pl
from jax.experimental.pallas import tpu as pltpu
from jax.sharding import PartitionSpec as P

F32 = jnp.float32
BF16 = jnp.bfloat16


def dot_f32(left, right, dims):
    return lax.dot_general(
        left, right, (dims, ((), ())), precision=lax.Precision.HIGHEST, preferred_element_type=F32
    )


def widen(column, lanes):
    return jnp.concatenate([column] * (lanes // 128), axis=1)


SIZE = 64
PANEL = 16


def factor_block(block):
    lane = lax.broadcasted_iota(jnp.int32, (8, 2 * SIZE), 1)
    sub = lax.broadcasted_iota(jnp.int32, (8, 2 * SIZE), 0)
    tiles = []
    for t in range(SIZE // 8):
        unit = (lane == sub + (8 * t + SIZE)).astype(F32)
        part = jnp.concatenate([block[8 * t : 8 * t + 8], jnp.zeros((8, SIZE), F32)], axis=1)
        tiles.append(part + unit)
    count = len(tiles)
    pivots = [jnp.ones((8, 2 * SIZE), F32) for _ in range(count)]
    for base in range(0, SIZE, PANEL):
        first = base // 8
        cols = [
            [None] * first
            + [jnp.broadcast_to(tiles[t][:, base + j : base + j + 1], (8, 2 * SIZE)) for t in range(first, count)]
            for j in range(PANEL)
        ]
        for j in range(PANEL):
            k = base + j
            row, here = k % 8, k // 8
            pivot = cols[j][here][row : row + 1]
            inverse = 1.0 / pivot
            pivots[here] = jnp.where(sub == row, pivot, pivots[here])
            scale = [None] * count
            for t in range(here, count):
                scale[t] = cols[j][t] * inverse
            scale[here] = jnp.where(sub > row, scale[here], 0.0)
            for later in range(j + 1, PANEL):
                value = cols[later][here][row : row + 1]
                for t in range(here, count):
                    cols[later][t] = cols[later][t] - scale[t] * value
            line = tiles[here][row : row + 1]
            for t in range(here, count):
                tiles[t] = tiles[t] - scale[t] * line
    done = []
    for t in range(count):
        keep = (lane >= SIZE) | (lane >= sub + 8 * t)
        done.append(jnp.where(keep, tiles[t] * lax.rsqrt(pivots[t]), 0.0))
    return jnp.concatenate(done, axis=0)


def halves(value):
    high = value.astype(BF16)
    return high, (value - high.astype(F32)).astype(BF16)


def dot_split(left, right, dims):
    (a, b), (c, d) = left, right

    def one(x, y):
        return lax.dot_general(x, y, (dims, ((), ())), preferred_element_type=F32)

    return one(a, c) + (one(a, d) + one(b, c))


def dot_rows(left, right):
    (a, b), (c, d) = left, right
    tall = jnp.concatenate([a, a, b], axis=0)
    other = jnp.concatenate([c, d, c], axis=0)
    return lax.dot_general(tall, other, (((0,), (0,)), ((), ())), preferred_element_type=F32)


def lanes(pair, start, stop):
    return tuple(part[:, start:stop] for part in pair)


def finish_kernel(particles, gram, coeffs, scores, factor, work, side, high, low):
    order = coeffs.shape[1]
    middle = order // 2
    for h in range(2):
        work[:, h * middle : (h + 1) * middle] = gram[:, h].reshape(order, middle) * (1.0 / particles)
    spot = lax.broadcasted_iota(jnp.int32, (order, order), 0)
    side[...] = (spot == lax.broadcasted_iota(jnp.int32, (order, order), 1)).astype(F32)
    high[...], low[...] = halves(coeffs[...])

    for start in range(0, order, SIZE):
        stop = start + SIZE
        both = factor_block(work[start:stop, start:stop])
        upper, lower = both[:, :SIZE], halves(both[:, SIZE:])
        if start:
            factor[start:stop, :start] = jnp.zeros((SIZE, start), F32)
        factor[start:stop, start:stop] = upper
        reach = -(-stop // 128) * 128
        base = stop // 128 * 128
        if stop < order:
            row_work = dot_split(lower, halves(work[start:stop, base:]), ((1,), (0,)))
            factor[start:stop, stop:] = row_work[:, stop - base :]
            cut = halves(row_work)
            near = lanes(cut, 0, 128)
            work[stop : base + 128, base:] = work[stop : base + 128, base:] - dot_rows(near, cut)[stop - base :]
        row_side = dot_split(lower, halves(side[start:stop, :reach]), ((1,), (0,)))
        side[start:stop, :reach] = row_side
        if stop < order:
            aside = halves(row_side)
            side[stop : base + 128, :reach] = side[stop : base + 128, :reach] - dot_rows(near, aside)[stop - base :]
            if base + 128 < order:
                rest = lanes(cut, 128, order - base)
                work[base + 128 :, base + 128 :] = work[base + 128 :, base + 128 :] - dot_rows(rest, rest)
                side[base + 128 :, :reach] = side[base + 128 :, :reach] - dot_rows(rest, aside)
        if stop % 128 == 0:
            columns = slice(stop - 128, stop)
            scores[:, columns] = dot_split(
                (high[:, :stop], low[:, :stop]), halves(side[columns, :stop]), ((1,), (1,))
            )


def finish(gram, coeffs, particles):
    order = coeffs.shape[1]
    return pl.pallas_call(
        functools.partial(finish_kernel, particles),
        in_specs=[pl.BlockSpec(memory_space=pltpu.VMEM)] * 2,
        out_specs=[pl.BlockSpec(memory_space=pltpu.VMEM)] * 2,
        out_shape=[jax.ShapeDtypeStruct(coeffs.shape, F32), jax.ShapeDtypeStruct((order, order), F32)],
        scratch_shapes=[pltpu.VMEM((order, order), F32)] * 2 + [pltpu.VMEM(coeffs.shape, BF16)] * 2,
        name="finish",
    )(gram, coeffs)


MESH = pl.DeviceIdType.MESH
BLOCKS = 3


def blocks_of(rows):
    first, second = rows * 5 // 14 // 32 * 32, rows * 5 // 14 // 32 * 32
    return first, second, rows - first - second


def gather_kernel(n_rows, n_dom, chunk, images, panels, means, table, pose, group, coeffs, gram, *scratch):
    img, pan, mea, tab, mark, mask, acc, part, near, held, far, wide, give, take, sems = scratch
    row, dom = lax.axis_index("rows"), lax.axis_index("dom")
    side, pair = row % 2, row // 2
    other = 1 - side
    partner = pair * 2 + other
    across = (1 - pair) * 2 + other
    own = (side + pair) % 2
    rows, pixels = images.shape
    bins, groups = panels.shape[0], table.shape[0]
    order = panels.shape[2]
    steps = pixels // chunk
    sizes = blocks_of(rows)
    starts = (0, sizes[0], sizes[0] + sizes[1])
    world = n_rows * n_dom
    ring = 2 * n_dom
    spot = dom * 2 + side
    flat = dom * n_rows + row
    piece = order // (2 * ring)
    links = 2 + steps * (bins + BLOCKS)
    pair_send, pair_recv, far_send, far_recv, back_send, back_recv = range(links, links + 6 * BLOCKS, BLOCKS)
    dom_send, dom_recv, all_send, all_recv = range(links + 6 * BLOCKS, links + 6 * BLOCKS + 4)

    def to(source, target, send, recv, place):
        return pltpu.make_async_remote_copy(
            src_ref=source, dst_ref=target, send_sem=sems.at[send], recv_sem=sems.at[recv], device_id=place, device_id_type=MESH
        )

    def local(source, target, sem):
        copy = pltpu.make_async_copy(source, target, sems.at[sem])
        copy.start()
        return copy

    small = [local(table, tab, 0), local(means, mea, 1)]
    weights, pictures = [], [[] for _ in range(BLOCKS)]
    for b in range(BLOCKS):
        for k in range(steps):
            px, at = pl.ds(k * chunk, chunk), pl.ds(starts[b], sizes[b])
            if b == 0:
                weights.append([local(panels.at[w, px], pan.at[w, px], 2 + w * steps + k) for w in range(bins)])
            pictures[b].append(local(images.at[at, px], img.at[at, px], 2 + (bins + b) * steps + k))

    barrier = pltpu.get_barrier_semaphore()

    def greet(step, carry):
        there = (flat + step) % world
        pl.semaphore_signal(
            barrier, inc=1, device_id=(there // n_rows, there % n_rows), device_id_type=MESH
        )
        return carry

    lax.fori_loop(1, world, greet, 0)
    gram[ring:, 0] = jnp.zeros((ring, piece, order // 2), F32)

    mark[...] = jnp.transpose(jnp.broadcast_to(group[...].astype(F32), (128, rows))).astype(jnp.int32)
    mask[...] = jnp.transpose(jnp.broadcast_to(pose[...].astype(F32), (128, rows)))
    for copy in small:
        copy.wait()

    def project(b, k):
        at, px = pl.ds(starts[b], sizes[b]), pl.ds(k * chunk, chunk)
        if b == 0:
            for copy in weights[k]:
                copy.wait()
        pictures[b][k].wait()
        lines = []
        for r in range(starts[b], starts[b] + sizes[b], 8):
            name = widen(mark[r : r + 8, :], chunk)
            line = None
            for base in range(0, groups, 8):
                found = jnp.take_along_axis(tab[base : base + 8, px], name % 8, axis=0, mode="promise_in_bounds")
                line = found if line is None else jnp.where(name >= base, found, line)
            lines.append(line)
        ctf = jnp.concatenate(lines, axis=0)
        second = widen(mask[at, :], chunk) > 0.5
        mean = jnp.where(second, mea[1:2, px], mea[0:1, px])
        weighted = (ctf * (img[at, px].astype(F32) - ctf * mean)).astype(BF16)
        for which in range(2):
            value = jnp.dot(weighted, pan[which, px, :], preferred_element_type=F32)
            if k:
                value = acc[which, : sizes[b], :] + value
            acc[which, : sizes[b], :] = value

    def mine(b, which):
        half = sizes[b] // 2
        return pl.ds(pl.multiple_of(starts[b] + which * half, 8), half)

    first, second, third = [], [], []

    def pair_start(b):
        at, size = pl.ds(starts[b], sizes[b]), sizes[b]
        part[at, :] = jnp.where(widen(mask[at, :], order) > 0.5, acc[1, :size, :], acc[0, :size, :])
        if b == 0:
            pl.semaphore_wait(barrier, world - 1)
        first.append(to(part.at[mine(b, 1 - own)], near.at[mine(b, 0)], pair_send + b, pair_recv + b, (dom, partner)))
        first[b].start()

    def pair_finish(b):
        first[b].wait_recv()
        held[mine(b, 0), :] = part[mine(b, own), :] + near[mine(b, 0), :]
        second.append(to(held.at[mine(b, 0)], far.at[mine(b, 0)], far_send + b, far_recv + b, (dom, across)))
        second[b].start()

    columns = pl.ds(pl.multiple_of(pair * (order // 2), 128), order // 2)

    def square(b):
        second[b].wait_recv()
        coeffs[mine(b, own), :] = held[mine(b, 0), :] + far[mine(b, 0), :]
        ours = coeffs.at[mine(b, own)]
        third.append(to(ours, ours, back_send + b, back_recv + b, (dom, partner)))
        third[b].start()
        return dot_rows(halves(coeffs[mine(b, own), columns]), halves(coeffs[mine(b, own), :]))

    for b in range(BLOCKS):
        for k in range(steps):
            project(b, k)
            if b and k == min(2, steps - 1):
                pair_finish(b - 1)
        pair_start(b)
    pair_finish(BLOCKS - 1)
    wide[...] = square(0)
    for b in range(1, BLOCKS):
        wide[...] += square(b)
    left = order // 2
    for j in range(ring):
        give[j, 0] = wide[j * piece : (j + 1) * piece, :left]
        give[j, 1] = wide[j * piece : (j + 1) * piece, left:]
    index = pair * ring + spot

    def part_of(ref, place, upper):
        return ref.at[place] if upper else ref.at[place, 1]

    def deal(step, upper):
        there = (spot + step) % ring
        place = (there // 2, pair * 2 + there % 2)
        return to(part_of(give, there, upper), part_of(take, spot, upper), dom_send, dom_recv, place)

    def spread(step, upper):
        there = (flat + step) % world
        ours = part_of(gram, index, upper)
        return to(ours, ours, all_send, all_recv + (0 if upper else 1), (there // n_rows, there % n_rows))

    def each(count, action):
        def one(step, carry):
            action(step)
            return carry

        if count <= 32:
            for step in range(1, count):
                action(step)
        else:
            lax.fori_loop(1, count, one, 0)

    def many(ref, count, upper, send, recv):
        those = part_of(ref, pl.ds(0, count), upper)
        return to(those, those, send, recv, (dom, partner))

    def exchange(upper):
        each(ring, lambda step: deal(step, upper).start())
        take[spot] = give[spot]
        dealt = many(take, ring - 1, upper, dom_send, dom_recv)
        dealt.wait_recv()
        for h in range(0 if upper else 1, 2):
            total = take[0, h]
            for j in range(1, ring):
                total = total + take[j, h]
            gram[index, h] = total
        each(world, lambda step: spread(step, upper).start())
        dealt.wait_send()
        many(gram, ring - 1 if upper else ring, True, all_send, all_recv).wait_recv()
        many(gram, ring if upper else ring - 1, False, all_send, all_recv + 1).wait_recv()
        many(gram, world - 1, upper, all_send, all_recv).wait_send()

    @pl.when(pair == 0)
    def _():
        exchange(True)

    @pl.when(pair == 1)
    def _():
        exchange(False)

    for copy in third:
        copy.wait_recv()
    for copy in first + second + third:
        copy.wait_send()


def gather(images, panels, means, table, pose, group):
    n_rows, n_dom = lax.axis_size("rows"), lax.axis_size("dom")
    rows, pixels = images.shape
    bins, _, order = panels.shape
    chunk = 1280 if pixels % 1280 == 0 else 128
    steps = pixels // chunk
    block = max(blocks_of(rows))
    ring = 2 * n_dom
    piece = order // (2 * ring)
    swap = pltpu.VMEM((rows, order), F32)
    coeffs, gram = pl.pallas_call(
        functools.partial(gather_kernel, n_rows, n_dom, chunk),
        in_specs=[pl.BlockSpec(memory_space=pltpu.HBM)] * 4 + [pl.BlockSpec(memory_space=pltpu.VMEM)] * 2,
        out_specs=[pl.BlockSpec(memory_space=pltpu.VMEM)] * 2,
        out_shape=[
            pltpu.VMEM((rows, order), F32),
            pltpu.VMEM((2 * ring, 2, piece, order // 2), F32),
        ],
        scratch_shapes=[
            pltpu.VMEM(images.shape, BF16),
            pltpu.VMEM(panels.shape, BF16),
            pltpu.VMEM(means.shape, F32),
            pltpu.VMEM(table.shape, F32),
            pltpu.VMEM((rows, 128), jnp.int32),
            pltpu.VMEM((rows, 128), F32),
            pltpu.VMEM((bins, block, order), F32),
            pltpu.VMEM((rows, order), F32),
            swap,
            swap,
            swap,
            pltpu.VMEM((order // 2, order), F32),
            pltpu.VMEM((ring, 2, piece, order // 2), F32),
            pltpu.VMEM((ring, 2, piece, order // 2), F32),
            pltpu.SemaphoreType.DMA((2 + steps * (bins + BLOCKS) + 6 * BLOCKS + 5,)),
        ],
        compiler_params=pltpu.CompilerParams(
            collective_id=0, has_side_effects=True, vmem_limit_bytes=60 * 2**20
        ),
        name="gather",
    )(images, panels, means, table, pose.reshape(1, rows), group.reshape(1, rows))
    return coeffs, gram


def body(images, panels, mean_panels, ctf_table, pose_bin, ctf_group):
    particles = images.shape[0] * lax.axis_size("dom")
    coeffs, gram = gather(images, panels, mean_panels, ctf_table, pose_bin, ctf_group)
    return tuple(finish(pltpu.with_memory_space_constraint(gram, pltpu.VMEM), pltpu.with_memory_space_constraint(coeffs, pltpu.VMEM), particles))


def solution(mesh):
    placed = (
        P("dom", "rows"),
        P("dom", "rows", None),
        P("dom", "rows"),
        P(None, "rows"),
        P("dom"),
        P("dom"),
    )
    return jax.shard_map(
        body, mesh=mesh, in_specs=placed, out_specs=(P("dom", None), P()), check_vma=False
    )
```

```python
import functools

import jax
import jax.numpy as jnp
from jax import lax
from jax.experimental import pallas as pl
from jax.experimental.pallas import tpu as pltpu
from jax.sharding import PartitionSpec as P

F32 = jnp.float32
BF16 = jnp.bfloat16


def dot_f32(left, right, dims):
    return lax.dot_general(
        left, right, (dims, ((), ())), precision=lax.Precision.HIGHEST, preferred_element_type=F32
    )


def widen(column, lanes):
    return jnp.concatenate([column] * (lanes // 128), axis=1)


SIZE = 64
PANEL = 16


def factor_block(block):
    lane = lax.broadcasted_iota(jnp.int32, (8, 2 * SIZE), 1)
    sub = lax.broadcasted_iota(jnp.int32, (8, 2 * SIZE), 0)
    tiles = []
    for t in range(SIZE // 8):
        unit = (lane == sub + (8 * t + SIZE)).astype(F32)
        part = jnp.concatenate([block[8 * t : 8 * t + 8], jnp.zeros((8, SIZE), F32)], axis=1)
        tiles.append(part + unit)
    count = len(tiles)
    pivots = [jnp.ones((8, 2 * SIZE), F32) for _ in range(count)]
    for base in range(0, SIZE, PANEL):
        first = base // 8
        cols = [
            [None] * first
            + [jnp.broadcast_to(tiles[t][:, base + j : base + j + 1], (8, 2 * SIZE)) for t in range(first, count)]
            for j in range(PANEL)
        ]
        for j in range(PANEL):
            k = base + j
            row, here = k % 8, k // 8
            pivot = cols[j][here][row : row + 1]
            inverse = 1.0 / pivot
            pivots[here] = jnp.where(sub == row, pivot, pivots[here])
            scale = [None] * count
            for t in range(here, count):
                scale[t] = cols[j][t] * inverse
            scale[here] = jnp.where(sub > row, scale[here], 0.0)
            for later in range(j + 1, PANEL):
                value = cols[later][here][row : row + 1]
                for t in range(here, count):
                    cols[later][t] = cols[later][t] - scale[t] * value
            line = tiles[here][row : row + 1]
            for t in range(here, count):
                tiles[t] = tiles[t] - scale[t] * line
    done = []
    for t in range(count):
        keep = (lane >= SIZE) | (lane >= sub + 8 * t)
        done.append(jnp.where(keep, tiles[t] * lax.rsqrt(pivots[t]), 0.0))
    return jnp.concatenate(done, axis=0)


def halves(value):
    high = value.astype(BF16)
    return high, (value - high.astype(F32)).astype(BF16)


def dot_split(left, right, dims):
    (a, b), (c, d) = left, right

    def one(x, y):
        return lax.dot_general(x, y, (dims, ((), ())), preferred_element_type=F32)

    return one(a, c) + (one(a, d) + one(b, c))


def dot_rows(left, right):
    (a, b), (c, d) = left, right
    tall = jnp.concatenate([a, a, b], axis=0)
    other = jnp.concatenate([c, d, c], axis=0)
    return lax.dot_general(tall, other, (((0,), (0,)), ((), ())), preferred_element_type=F32)


def lanes(pair, start, stop):
    return tuple(part[:, start:stop] for part in pair)


def finish_kernel(particles, gram, high, low, scores, factor, work, side):
    order = high.shape[1]
    middle = order // 2
    for h in range(2):
        work[:, h * middle : (h + 1) * middle] = gram[:, h].reshape(order, middle) * (1.0 / particles)
    spot = lax.broadcasted_iota(jnp.int32, (order, order), 0)
    side[...] = (spot == lax.broadcasted_iota(jnp.int32, (order, order), 1)).astype(F32)

    for start in range(0, order, SIZE):
        stop = start + SIZE
        both = factor_block(work[start:stop, start:stop])
        upper, lower = both[:, :SIZE], halves(both[:, SIZE:])
        if start:
            factor[start:stop, :start] = jnp.zeros((SIZE, start), F32)
        factor[start:stop, start:stop] = upper
        reach = -(-stop // 128) * 128
        base = stop // 128 * 128
        if stop < order:
            row_work = dot_split(lower, halves(work[start:stop, base:]), ((1,), (0,)))
            factor[start:stop, stop:] = row_work[:, stop - base :]
            cut = halves(row_work)
            near = lanes(cut, 0, 128)
            work[stop : base + 128, base:] = work[stop : base + 128, base:] - dot_rows(near, cut)[stop - base :]
        row_side = dot_split(lower, halves(side[start:stop, :reach]), ((1,), (0,)))
        side[start:stop, :reach] = row_side
        if stop < order:
            aside = halves(row_side)
            side[stop : base + 128, :reach] = side[stop : base + 128, :reach] - dot_rows(near, aside)[stop - base :]
            if base + 128 < order:
                rest = lanes(cut, 128, order - base)
                work[base + 128 :, base + 128 :] = work[base + 128 :, base + 128 :] - dot_rows(rest, rest)
                side[base + 128 :, :reach] = side[base + 128 :, :reach] - dot_rows(rest, aside)
        if stop % 128 == 0:
            columns = slice(stop - 128, stop)
            scores[:, columns] = dot_split(
                (high[:, :stop], low[:, :stop]), halves(side[columns, :stop]), ((1,), (1,))
            )


def finish(gram, high, low, particles):
    order = high.shape[1]
    return pl.pallas_call(
        functools.partial(finish_kernel, particles),
        in_specs=[pl.BlockSpec(memory_space=pltpu.VMEM)] * 3,
        out_specs=[pl.BlockSpec(memory_space=pltpu.VMEM)] * 2,
        out_shape=[jax.ShapeDtypeStruct(high.shape, F32), jax.ShapeDtypeStruct((order, order), F32)],
        scratch_shapes=[pltpu.VMEM((order, order), F32)] * 2,
        name="finish",
    )(gram, high, low)


MESH = pl.DeviceIdType.MESH
BLOCKS = 3


def blocks_of(rows):
    first, second = rows * 5 // 14 // 32 * 32, rows * 5 // 14 // 32 * 32
    return first, second, rows - first - second


def gather_kernel(n_rows, n_dom, chunk, images, panels, means, table, pose, group, high, low, gram, *scratch):
    img, pan, mea, tab, mark, mask, acc, part, near, held, far, wide, give, take, coeffs, sems = scratch
    row, dom = lax.axis_index("rows"), lax.axis_index("dom")
    side, pair = row % 2, row // 2
    other = 1 - side
    partner = pair * 2 + other
    across = (1 - pair) * 2 + other
    own = (side + pair) % 2
    rows, pixels = images.shape
    bins, groups = panels.shape[0], table.shape[0]
    order = panels.shape[2]
    steps = pixels // chunk
    sizes = blocks_of(rows)
    starts = (0, sizes[0], sizes[0] + sizes[1])
    world = n_rows * n_dom
    ring = 2 * n_dom
    spot = dom * 2 + side
    flat = dom * n_rows + row
    piece = order // (2 * ring)
    links = 2 + steps * (bins + BLOCKS)
    pair_send, pair_recv, far_send, far_recv, back_send, back_recv = range(links, links + 6 * BLOCKS, BLOCKS)
    dom_send, dom_recv, all_send, all_recv = range(links + 6 * BLOCKS, links + 6 * BLOCKS + 4)

    def to(source, target, send, recv, place):
        return pltpu.make_async_remote_copy(
            src_ref=source, dst_ref=target, send_sem=sems.at[send], recv_sem=sems.at[recv], device_id=place, device_id_type=MESH
        )

    def local(source, target, sem):
        copy = pltpu.make_async_copy(source, target, sems.at[sem])
        copy.start()
        return copy

    small = [local(table, tab, 0), local(means, mea, 1)]
    weights, pictures = [], [[] for _ in range(BLOCKS)]
    for b in range(BLOCKS):
        for k in range(steps):
            px, at = pl.ds(k * chunk, chunk), pl.ds(starts[b], sizes[b])
            if b == 0:
                weights.append([local(panels.at[w, px], pan.at[w, px], 2 + w * steps + k) for w in range(bins)])
            pictures[b].append(local(images.at[at, px], img.at[at, px], 2 + (bins + b) * steps + k))

    barrier = pltpu.get_barrier_semaphore()

    def greet(step, carry):
        there = (flat + step) % world
        pl.semaphore_signal(
            barrier, inc=1, device_id=(there // n_rows, there % n_rows), device_id_type=MESH
        )
        return carry

    lax.fori_loop(1, world, greet, 0)
    gram[ring:, 0] = jnp.zeros((ring, piece, order // 2), F32)

    mark[...] = jnp.transpose(jnp.broadcast_to(group[...].astype(F32), (128, rows))).astype(jnp.int32)
    mask[...] = jnp.transpose(jnp.broadcast_to(pose[...].astype(F32), (128, rows)))
    for copy in small:
        copy.wait()

    def project(b, k):
        at, px = pl.ds(starts[b], sizes[b]), pl.ds(k * chunk, chunk)
        if b == 0:
            for copy in weights[k]:
                copy.wait()
        pictures[b][k].wait()
        lines = []
        for r in range(starts[b], starts[b] + sizes[b], 8):
            name = widen(mark[r : r + 8, :], chunk)
            line = None
            for base in range(0, groups, 8):
                found = jnp.take_along_axis(tab[base : base + 8, px], name % 8, axis=0, mode="promise_in_bounds")
                line = found if line is None else jnp.where(name >= base, found, line)
            lines.append(line)
        ctf = jnp.concatenate(lines, axis=0)
        second = widen(mask[at, :], chunk) > 0.5
        mean = jnp.where(second, mea[1:2, px], mea[0:1, px])
        weighted = (ctf * (img[at, px].astype(F32) - ctf * mean)).astype(BF16)
        for which in range(2):
            value = jnp.dot(weighted, pan[which, px, :], preferred_element_type=F32)
            if k:
                value = acc[which, : sizes[b], :] + value
            acc[which, : sizes[b], :] = value

    def mine(b, which):
        half = sizes[b] // 2
        return pl.ds(pl.multiple_of(starts[b] + which * half, 8), half)

    first, second, third = [], [], []

    def pair_start(b):
        at, size = pl.ds(starts[b], sizes[b]), sizes[b]
        part[at, :] = jnp.where(widen(mask[at, :], order) > 0.5, acc[1, :size, :], acc[0, :size, :])
        if b == 0:
            pl.semaphore_wait(barrier, world - 1)
        first.append(to(part.at[mine(b, 1 - own)], near.at[mine(b, 0)], pair_send + b, pair_recv + b, (dom, partner)))
        first[b].start()

    def pair_finish(b):
        first[b].wait_recv()
        held[mine(b, 0), :] = part[mine(b, own), :] + near[mine(b, 0), :]
        second.append(to(held.at[mine(b, 0)], far.at[mine(b, 0)], far_send + b, far_recv + b, (dom, across)))
        second[b].start()

    columns = pl.ds(pl.multiple_of(pair * (order // 2), 128), order // 2)

    def square(b):
        second[b].wait_recv()
        coeffs[mine(b, own), :] = held[mine(b, 0), :] + far[mine(b, 0), :]
        ours = coeffs.at[mine(b, own)]
        third.append(to(ours, ours, back_send + b, back_recv + b, (dom, partner)))
        third[b].start()
        return dot_rows(halves(coeffs[mine(b, own), columns]), halves(coeffs[mine(b, own), :]))

    for b in range(BLOCKS):
        for k in range(steps):
            project(b, k)
            if b and k == min(2, steps - 1):
                pair_finish(b - 1)
        pair_start(b)
    pair_finish(BLOCKS - 1)
    wide[...] = square(0)
    for b in range(1, BLOCKS):
        wide[...] += square(b)
    left = order // 2
    for j in range(ring):
        give[j, 0] = wide[j * piece : (j + 1) * piece, :left]
        give[j, 1] = wide[j * piece : (j + 1) * piece, left:]
    index = pair * ring + spot

    def part_of(ref, place, upper):
        return ref.at[place] if upper else ref.at[place, 1]

    def deal(step, upper):
        there = (spot + step) % ring
        place = (there // 2, pair * 2 + there % 2)
        return to(part_of(give, there, upper), part_of(take, spot, upper), dom_send, dom_recv, place)

    def spread(step, upper):
        there = (flat + step) % world
        ours = part_of(gram, index, upper)
        return to(ours, ours, all_send, all_recv + (0 if upper else 1), (there // n_rows, there % n_rows))

    def each(count, action):
        def one(step, carry):
            action(step)
            return carry

        if count <= 32:
            for step in range(1, count):
                action(step)
        else:
            lax.fori_loop(1, count, one, 0)

    def many(ref, count, upper, send, recv):
        those = part_of(ref, pl.ds(0, count), upper)
        return to(those, those, send, recv, (dom, partner))

    def exchange(upper):
        each(ring, lambda step: deal(step, upper).start())
        take[spot] = give[spot]
        dealt = many(take, ring - 1, upper, dom_send, dom_recv)
        dealt.wait_recv()
        for h in range(0 if upper else 1, 2):
            total = take[0, h]
            for j in range(1, ring):
                total = total + take[j, h]
            gram[index, h] = total
        each(world, lambda step: spread(step, upper).start())
        dealt.wait_send()
        for copy in third:
            copy.wait_recv()
        high[...], low[...] = halves(coeffs[...])
        many(gram, ring - 1 if upper else ring, True, all_send, all_recv).wait_recv()
        many(gram, ring if upper else ring - 1, False, all_send, all_recv + 1).wait_recv()
        many(gram, world - 1, upper, all_send, all_recv).wait_send()

    @pl.when(pair == 0)
    def _():
        exchange(True)

    @pl.when(pair == 1)
    def _():
        exchange(False)

    for copy in first + second + third:
        copy.wait_send()


def gather(images, panels, means, table, pose, group):
    n_rows, n_dom = lax.axis_size("rows"), lax.axis_size("dom")
    rows, pixels = images.shape
    bins, _, order = panels.shape
    chunk = 1280 if pixels % 1280 == 0 else 128
    steps = pixels // chunk
    block = max(blocks_of(rows))
    ring = 2 * n_dom
    piece = order // (2 * ring)
    swap = pltpu.VMEM((rows, order), F32)
    high, low, gram = pl.pallas_call(
        functools.partial(gather_kernel, n_rows, n_dom, chunk),
        in_specs=[pl.BlockSpec(memory_space=pltpu.HBM)] * 4 + [pl.BlockSpec(memory_space=pltpu.VMEM)] * 2,
        out_specs=[pl.BlockSpec(memory_space=pltpu.VMEM)] * 3,
        out_shape=[
            pltpu.VMEM((rows, order), BF16),
            pltpu.VMEM((rows, order), BF16),
            pltpu.VMEM((2 * ring, 2, piece, order // 2), F32),
        ],
        scratch_shapes=[
            pltpu.VMEM(images.shape, BF16),
            pltpu.VMEM(panels.shape, BF16),
            pltpu.VMEM(means.shape, F32),
            pltpu.VMEM(table.shape, F32),
            pltpu.VMEM((rows, 128), jnp.int32),
            pltpu.VMEM((rows, 128), F32),
            pltpu.VMEM((bins, block, order), F32),
            pltpu.VMEM((rows, order), F32),
            swap,
            swap,
            swap,
            pltpu.VMEM((order // 2, order), F32),
            pltpu.VMEM((ring, 2, piece, order // 2), F32),
            pltpu.VMEM((ring, 2, piece, order // 2), F32),
            pltpu.VMEM((rows, order), F32),
            pltpu.SemaphoreType.DMA((2 + steps * (bins + BLOCKS) + 6 * BLOCKS + 5,)),
        ],
        compiler_params=pltpu.CompilerParams(
            collective_id=0, has_side_effects=True, vmem_limit_bytes=60 * 2**20
        ),
        name="gather",
    )(images, panels, means, table, pose.reshape(1, rows), group.reshape(1, rows))
    return high, low, gram


def body(images, panels, mean_panels, ctf_table, pose_bin, ctf_group):
    particles = images.shape[0] * lax.axis_size("dom")
    high, low, gram = (
        pltpu.with_memory_space_constraint(part, pltpu.VMEM)
        for part in gather(images, panels, mean_panels, ctf_table, pose_bin, ctf_group)
    )
    return tuple(finish(gram, high, low, particles))


def solution(mesh):
    placed = (
        P("dom", "rows"),
        P("dom", "rows", None),
        P("dom", "rows"),
        P(None, "rows"),
        P("dom"),
        P("dom"),
    )
    return jax.shard_map(
        body, mesh=mesh, in_specs=placed, out_specs=(P("dom", None), P()), check_vma=False
    )
```
